32 devices in a mesh: groups: 2 (over y), ctx: 16 (over z, x, core).
Axes of the slice: x: 2, y: 2, z: 4, core: 2. Of those that a mesh axis runs over, the one named last changes fastest.
Arguments:
- queries: bfloat16 [4096, 1024], P(('groups', 'ctx')), parts along dimension 0, may hold values from -256 to 256
- key_rows: bfloat16 [4096, 1024], P(('groups', 'ctx')), parts along dimension 0, may hold values from -256 to 256
- value_rows: bfloat16 [4096, 1024], P(('groups', 'ctx')), parts along dimension 0, may hold values from -6 to 6
- write_strength: float32 [8, 4096], P(None, ('groups', 'ctx')), parts along dimension 1, may hold values from 0 to 1, as said below
- log_decay: float32 [8, 4096], P(None, ('groups', 'ctx')), parts along dimension 1, may hold values from -2 to 0, as said below
- level_gates: float32 [5, 8, 4096], P(None, None, ('groups', 'ctx')), parts along dimension 2, may hold values from 0.2 to 2
Outputs:
- layer_out: float32 [4096, 1024], P(('groups', 'ctx')), parts along dimension 0
The draws below stay inside these ranges and needn't reach their ends.
There are 2 independent parts, one for each index of `groups`. The reference program is written for one: setup_inputs(seed, part) draws one part's arguments, and reference() takes and returns one part's arrays. A program takes and returns all parts, laid end to end along the dimension named above; each array names one. Nothing has to cross between parts.
Inputs may be any that keep to these rules, and one draw needn't show every extreme that they name: `write_strength`: Positive. `log_decay`: never positive.
All inputs are finite; a program needn't handle non-finite values.
Results may differ from the reference program's by a relative error of at most 0.0003.
Values sent between devices are 32-bit elements; how exact they have to be, the bound alone decides.
No kernel may reach another device: no remote copies, remote signals or barrier semaphores. Data moves between devices by JAX's collectives and lax.ppermute only.
A program may use at most 64 MiB of HBM per device.

```python
import math
import jax
import jax.numpy as jnp
from jax import lax

HEAD_GROUP = 8
DK = 128
DV = 128
TOK_DEV = 128
TOKEN_COUNT = 2048
LEVELS = 4
N_CTX = 16


def head_plan(key):
    base_key = jax.random.fold_in(key, 9101)
    ranking = jax.random.permutation(jax.random.fold_in(base_key, 1), HEAD_GROUP)
    slow_count = HEAD_GROUP // 2
    fast_count = max(1, HEAD_GROUP // 4)
    slow_heads = ranking < slow_count
    fast_heads = (ranking >= slow_count) & (ranking < slow_count + fast_count)
    span_draw = jax.random.uniform(jax.random.fold_in(base_key, 2), (HEAD_GROUP,), jnp.float32)
    low_log = math.log(2.0 * TOK_DEV)
    high_log = math.log(max(4.0 * TOK_DEV, TOKEN_COUNT / 8.0))
    middle_span = jnp.exp(low_log + (high_log - low_log) * span_draw)
    memory_span = jnp.where(slow_heads, jnp.float32(TOKEN_COUNT), jnp.where(fast_heads, jnp.float32(40.0), middle_span))
    phase_draw = jax.random.uniform(jax.random.fold_in(base_key, 3), (HEAD_GROUP,), jnp.float32, 0.0, 2.0 * math.pi)
    return (fast_heads, memory_span, phase_draw)


def draw_write_strength(key, part):
    fast_heads, memory_span, phase_draw = head_plan(key)
    head_level = jax.random.uniform(jax.random.fold_in(key, 21), (HEAD_GROUP,), jnp.float32, 0.5, 1.5)
    random_noise = jax.random.uniform(jax.random.fold_in(key, 22), (HEAD_GROUP, TOKEN_COUNT), jnp.float32, 0.5, 1.5)
    head_base = jnp.where(fast_heads, 0.4 * head_level, 0.5 * DK / memory_span * head_level)
    return jnp.minimum(head_base[:, None] * random_noise, 0.9)


def draw_log_decay(key, part):
    fast_heads, memory_span, phase_draw = head_plan(key)
    places = jnp.arange(TOKEN_COUNT, dtype=jnp.float32)
    sine_pattern = jnp.exp(0.7 * jnp.sin(6.0 * math.pi * places[None, :] / TOKEN_COUNT + phase_draw[:, None]))
    random_noise = jnp.exp(jax.random.uniform(jax.random.fold_in(key, 31), (HEAD_GROUP, TOKEN_COUNT), jnp.float32, -0.5, 0.5))
    fast_rate = jax.random.uniform(jax.random.fold_in(key, 32), (HEAD_GROUP,), jnp.float32, 0.8, 1.25) / 40.0
    slow_rate = jax.random.uniform(jax.random.fold_in(key, 33), (HEAD_GROUP,), jnp.float32, 0.05, 0.2) / memory_span
    head_decay_rate = jnp.where(fast_heads, fast_rate, slow_rate)
    spike_choice_index = jax.random.uniform(jax.random.fold_in(key, 34), (HEAD_GROUP, TOKEN_COUNT), jnp.float32)
    spike_keep_mask = jax.random.uniform(jax.random.fold_in(key, 35), (HEAD_GROUP, TOKEN_COUNT), jnp.float32, 0.5, 0.8)
    spike_extra_term = jnp.where(spike_choice_index < 2.0 / TOKEN_COUNT, jnp.log(spike_keep_mask), 0.0)
    return -head_decay_rate[:, None] * sine_pattern * random_noise + spike_extra_term


def scaled_rows(key):
    entries = jnp.clip(jax.random.normal(jax.random.fold_in(key, 1), (TOKEN_COUNT, HEAD_GROUP * DK), jnp.float32), -5.0, 5.0)
    row_top = math.log(10.0)
    row_scale = jnp.exp(jax.random.uniform(jax.random.fold_in(key, 2), (TOKEN_COUNT, 1), jnp.float32, 0.0, row_top))
    column_scale = jnp.exp(jax.random.uniform(jax.random.fold_in(key, 3), (1, HEAD_GROUP * DK), jnp.float32, 0.0, math.log(3.0)))
    return (entries * row_scale * column_scale).astype(jnp.bfloat16)


def draw_queries(key, part):
    return scaled_rows(jax.random.fold_in(key, 501))


def draw_key_rows(key, part):
    return scaled_rows(jax.random.fold_in(key, 502))


def block_levels(own_key, dims, cuts, least, largest):
    def one(position, shards_of):
        heights = jax.random.uniform(jax.random.fold_in(jax.random.fold_in(own_key, 6), position), (shards_of,), jnp.float32, least / len(cuts), largest / len(cuts))
        return jnp.repeat(jnp.exp(heights), dims[position] // shards_of).reshape((-1,) + (1,) * (len(dims) - position - 1))

    gain = one(*cuts[0])
    for cut in cuts[1:]:
        gain = gain * one(*cut)
    return gain


def noise(stream_key, extent, deviation, limit, shards=(), kind=jnp.bfloat16):
    values = deviation * jax.random.normal(stream_key, extent, jnp.float32)
    if shards:
        values = values * block_levels(stream_key, extent, shards, -0.22, 0.18)
    return jnp.clip(values, -limit, limit).astype(kind)


def setup_inputs(seed: int = 0, part: int = 0) -> dict:
    streams_of = jax.random.split(jax.random.key(seed), 7)
    own_keys = jax.random.split(jax.random.fold_in(streams_of[6], part), 7)
    queries = draw_queries(jax.random.fold_in(jax.random.fold_in(streams_of[6], part), 71), part)
    key_rows = draw_key_rows(jax.random.fold_in(jax.random.fold_in(streams_of[6], part), 71), part)
    value_rows = noise(own_keys[2], (TOKEN_COUNT, HEAD_GROUP * DV), 1.0, 6.0, ((0, 16),))
    write_strength = draw_write_strength(jax.random.fold_in(jax.random.fold_in(streams_of[6], part), 71), part)
    log_decay = draw_log_decay(jax.random.fold_in(jax.random.fold_in(streams_of[6], part), 71), part)
    level_gates = jnp.clip(jnp.exp(math.log(2.0) - 2.3025851 * jax.random.uniform(own_keys[5], (LEVELS + 1, HEAD_GROUP, TOKEN_COUNT), jnp.float32) ** block_levels(own_keys[5], (LEVELS + 1, HEAD_GROUP, TOKEN_COUNT), ((2, 16),), -0.2, 0.2)), 0.2, 2.0)
    return dict(queries=queries, key_rows=key_rows, value_rows=value_rows, write_strength=write_strength, log_decay=log_decay, level_gates=level_gates)


norm_eps = 1e-06

def unit_rows(matrix):
    return matrix * lax.rsqrt(lax.optimization_barrier(jnp.sum(matrix * matrix, axis=-1, keepdims=True)) + norm_eps)

def head_major(block, head_count):
    count = block.shape[0]
    return block.astype(jnp.float32).reshape(count, head_count, -1).transpose(1, 0, 2)

def block_solve(queries, key_rows, value_rows, write_strength, log_decay):
    head_count = write_strength.shape[0]
    count = write_strength.shape[1]
    query_unit = unit_rows(head_major(queries, head_count))
    key_unit = unit_rows(head_major(key_rows, head_count))
    value_head = head_major(value_rows, head_count)
    key_width = key_unit.shape[2]
    running = jnp.cumsum(log_decay, axis=1)
    row_index = lax.broadcasted_iota(jnp.int32, (count, count), 0)
    col_index = lax.broadcasted_iota(jnp.int32, (count, count), 1)
    lower_incl = (row_index >= col_index)[None]
    lower_strict = (row_index > col_index)[None]
    gap_log = jnp.where(lower_incl, running[:, :, None] - running[:, None, :], 0.0)
    decay_ratio = jnp.where(lower_incl, jnp.exp(gap_log), 0.0)
    key_gram = jnp.einsum('htk,hsk->hts', key_unit, key_unit, precision=lax.Precision.HIGHEST)
    identity = jnp.eye(count, dtype=jnp.float32)
    tri_matrix = identity[None] + jnp.where(lower_strict, write_strength[:, :, None] * key_gram * decay_ratio, 0.0)
    growth = jnp.exp(running)
    right_side = jnp.concatenate([(write_strength * growth)[:, :, None] * key_unit, write_strength[:, :, None] * value_head], axis=2)
    solved = jax.scipy.linalg.solve_triangular(tri_matrix, right_side, lower=True, unit_diagonal=True)
    erase_rows = solved[:, :, :key_width]
    written_value_rows = solved[:, :, key_width:]
    query_gram = jnp.einsum('htk,hsk->hts', query_unit, key_unit, precision=lax.Precision.HIGHEST) * decay_ratio
    local_read = jnp.einsum('hts,hsv->htv', query_gram, written_value_rows, precision=lax.Precision.HIGHEST)
    effective_query = growth[:, :, None] * query_unit - jnp.einsum('hts,hsk->htk', query_gram, erase_rows, precision=lax.Precision.HIGHEST)
    to_end = jnp.exp(running[:, -1:] - running)
    final_key_rows = key_unit * to_end[:, :, None]
    block_memory_state = jnp.einsum('gjz,gjn->gzn', final_key_rows, written_value_rows, precision=lax.Precision.HIGHEST)
    key_eye = jnp.eye(key_width, dtype=jnp.float32)
    block_trans = growth[:, -1][:, None, None] * key_eye[None] - jnp.einsum('hsk,hsj->hkj', final_key_rows, erase_rows, precision=lax.Precision.HIGHEST)
    return (local_read, effective_query, block_memory_state, block_trans)

def reference(queries, key_rows, value_rows, write_strength, log_decay, level_gates):
    query_blocks = queries.reshape(N_CTX, TOK_DEV, HEAD_GROUP * DK)
    key_blocks = key_rows.reshape(N_CTX, TOK_DEV, HEAD_GROUP * DK)
    value_blocks = value_rows.reshape(N_CTX, TOK_DEV, HEAD_GROUP * DV)
    strength_blocks = write_strength.reshape(HEAD_GROUP, N_CTX, TOK_DEV).transpose(1, 0, 2)
    decay_blocks = log_decay.reshape(HEAD_GROUP, N_CTX, TOK_DEV).transpose(1, 0, 2)
    gate_blocks = level_gates.reshape(LEVELS + 1, HEAD_GROUP, N_CTX, TOK_DEV).transpose(2, 0, 1, 3)
    powers = jnp.left_shift(jnp.int32(1), jnp.arange(LEVELS + 1, dtype=jnp.int32))

    def advance(carry, inputs):
        level_memory, device_num = carry
        query_part, key_part, value_part, strength_part, decay_part, gate_part = inputs
        local_read, effective_query, block_memory_state, block_trans = block_solve(query_part, key_part, value_part, strength_part, decay_part)
        level_terms = jnp.einsum('htk,lhkv->lhtv', effective_query, level_memory, precision=lax.Precision.HIGHEST)
        total = gate_part[0][:, :, None] * local_read + lax.optimization_barrier(jnp.sum(gate_part[1:][:, :, :, None] * level_terms, axis=0))
        block_out = total.transpose(1, 0, 2).reshape(TOK_DEV, HEAD_GROUP * DV)
        following = device_num + jnp.int32(1)
        carried = jnp.einsum('hkj,lhjv->lhkv', block_trans, level_memory, precision=lax.Precision.HIGHEST)
        below_or_at = following % powers[:LEVELS] == 0
        strictly_below = following % powers[1:] == 0
        merged = lax.optimization_barrier(jnp.sum(jnp.where(below_or_at[:, None, None, None], carried, 0.0), axis=0)) + block_memory_state
        level_memory = jnp.where(strictly_below[:, None, None, None], 0.0, jnp.where(below_or_at[:, None, None, None], merged[None], carried))
        return ((level_memory, following), block_out)
    start_memory = jnp.zeros((LEVELS, HEAD_GROUP, DK, DV), dtype=jnp.float32)
    final_carry, outputs = lax.scan(advance, (start_memory, jnp.int32(0)), (query_blocks, key_blocks, value_blocks, strength_blocks, decay_blocks, gate_blocks))
    return outputs.reshape(TOKEN_COUNT, HEAD_GROUP * DV)
```

```python
import jax
import jax.numpy as jnp
from jax import lax
from jax.experimental import pallas as pl
from jax.experimental.pallas import tpu as pltpu
from jax.sharding import PartitionSpec as P

norm_eps = 1e-06
f32 = jnp.float32
bf16 = jnp.bfloat16


def parts(value):
    high = value.astype(bf16)
    return high, (value - high.astype(f32)).astype(bf16)


def mm(left, right, dims=((1,), (0,))):
    return lax.dot_general(left, right, (dims, ((), ())), preferred_element_type=f32)


def dot_ff(left, right):
    width = right.shape[1]
    left_parts = jnp.concatenate(parts(left), axis=1)
    right_row = jnp.concatenate(parts(right), axis=1)
    both = mm(left_parts, jnp.concatenate([right_row, right_row], axis=0))
    return both[:, :width] + both[:, width:]


def dot_fb(left, right):
    left_parts = jnp.concatenate(parts(left), axis=1)
    return mm(left_parts, jnp.concatenate([right, right], axis=0))


def dot_bf_t(left, right):
    width = right.shape[1]
    both = mm(left, jnp.concatenate(parts(right), axis=1), ((0,), (0,)))
    return both[:, :width] + both[:, width:]


def block_kernel(sel_ref, q_ref, k_ref, v_ref, beta_ref, decay_ref, gates_ref, tse_ref, local_ref):
    half = tse_ref.shape[0]
    count = q_ref.shape[0]
    width = q_ref.shape[1] // half
    heads = beta_ref.shape[0]
    upper = sel_ref[0] == 1

    def chosen_first(rows):
        return jnp.where(upper, pltpu.roll(rows, half, 0), rows)

    row = lax.broadcasted_iota(jnp.int32, (count, count), 0)
    col = lax.broadcasted_iota(jnp.int32, (count, count), 1)
    summing = jnp.where(row <= col, 1.0, 0.0).astype(bf16)
    decay = decay_ref[...]
    d1 = decay.astype(bf16)
    rest = decay - d1.astype(f32)
    d2 = rest.astype(bf16)
    d3 = (rest - d2.astype(f32)).astype(bf16)
    running = chosen_first(mm(d1, summing) + (mm(d2, summing) + mm(d3, summing)))
    beta = chosen_first(beta_ref[...])
    gate = chosen_first(gates_ref[0])
    growth = jnp.exp(running)
    to_end = jnp.exp(running[:, count - 1 :] - running)
    stack = jnp.concatenate(
        [running, beta, growth, to_end, gate, jnp.zeros((count - 5 * heads, count), f32)], axis=0
    )
    columns = stack.T

    def column(kind, head):
        return columns[:, kind * heads + head : kind * heads + head + 1]

    k_rows, q_rows, k_norm = [], [], jnp.zeros((count, count), f32)
    scales = []
    for j in range(half):
        lanes = slice(j * width, (j + 1) * width)
        kj = k_ref[:, lanes]
        qj = q_ref[:, lanes]
        kf = kj.astype(f32)
        qf = qj.astype(f32)
        k_scale = lax.rsqrt(jnp.sum(kf * kf, axis=1, keepdims=True) + norm_eps)
        q_scale = lax.rsqrt(jnp.sum(qf * qf, axis=1, keepdims=True) + norm_eps)
        k_norm = jnp.where(col == j, k_scale, k_norm)
        k_rows.append(kj)
        q_rows.append(qj)
        scales.append((k_scale, q_scale))
    k_norm_rows = k_norm.T

    lower_incl = row >= col
    nexts, inverses, query_grams = [], [], []
    for j in range(half):
        k_scale, q_scale = scales[j]
        kj = k_rows[j]
        run_row = running[j : j + 1]
        gap = jnp.where(lower_incl, column(0, j) - run_row, 0.0)
        ratio = jnp.where(lower_incl, jnp.exp(gap), 0.0) * k_norm_rows[j : j + 1]
        grams = mm(jnp.concatenate([kj, q_rows[j]], axis=0), kj, ((1,), (1,)))
        below = grams[:count] * ratio * (column(1, j) * k_scale)
        query_grams.append(grams[count:] * ratio * q_scale)
        nexts.append(below)
        first = jnp.where((row ^ col) == 1, below, 0.0)
        inverses.append(jnp.where(row == col, 1.0, jnp.where(row > col, -first, 0.0)))
    level = 1
    while (1 << level) < count:
        pair = ((row >> level) ^ (col >> level)) == 1
        pair = pair & (row > col)
        for j in range(half):
            link = jnp.where(pair, nexts[j], 0.0)
            inverse = inverses[j]
            inverses[j] = inverse - dot_ff(inverse, dot_ff(link, inverse))
        level += 1
    for j in range(half):
        lanes = slice(j * width, (j + 1) * width)
        k_scale, q_scale = scales[j]
        kj = k_rows[j]
        inverse = inverses[j]
        from_query = dot_ff(query_grams[j], inverse)
        from_key = dot_bf_t(kj, inverse * (column(3, j) * k_scale))
        both = jnp.concatenate([from_query, from_key], axis=0)
        beta_row = beta[j : j + 1]
        written = dot_fb(both * beta_row, v_ref[:, lanes])
        erased = dot_fb(both * (beta_row * growth[j : j + 1] * k_norm_rows[j : j + 1]), kj)
        local_ref[:, lanes] = column(4, j) * written[:count]
        last = growth[j : j + 1, count - 1 :]
        diagonal = jnp.where(row[:width, :width] == col[:width, :width], last, 0.0)
        tse_ref[j, :, :width] = diagonal - erased[count:]
        tse_ref[j, :, width : 2 * width] = written[count:]
        tse_ref[j, :, 2 * width :] = (column(2, j) * q_scale) * q_rows[j].astype(f32) - erased[:count]


def composed(later, earlier, width):
    both = dot_ff(later[:, :width], earlier)
    return jnp.concatenate([both[:, :width], both[:, width:] + later[:, width:]], axis=1)


def pair_kernel(sel_ref, own_ref, other_ref, send_ref, keep_ref):
    width = own_ref.shape[1]
    share = send_ref.shape[0]
    odd = sel_ref[0] == 1
    x = sel_ref[1]
    for target, base in ((send_ref, (1 - x) * share), (keep_ref, x * share)):
        for j in range(share):
            own = own_ref[base + j, :, : 2 * width]
            other = other_ref[base + j, :, : 2 * width]
            later = jnp.where(odd, own, other)
            earlier = jnp.where(odd, other, own)
            target[j] = composed(later, earlier, width)


def first_read_kernel(sel_ref, own_ref, other_ref, gates_ref, gates_other_ref, eff_ref, read_ref, cols_ref):
    half, width = own_ref.shape[:2]
    count = own_ref.shape[1]
    levels, heads = gates_ref.shape[0] - 1, gates_ref.shape[1]
    odd = sel_ref[0] == 1

    def chosen_first(rows):
        return jnp.where(odd, pltpu.roll(rows, half, 0), rows)

    even_gates, odd_gates = [], []
    for b in range(levels):
        mine = chosen_first(gates_ref[b + 1])
        others = chosen_first(gates_other_ref[b + 1])
        even_gates.append(jnp.where(odd, others, mine))
        odd_gates.append(jnp.where(odd, mine, others))
    filler = [jnp.zeros((count - heads * levels, count), f32)]
    even_cols = jnp.concatenate(even_gates + filler, axis=0).T
    odd_cols = jnp.concatenate(odd_gates + filler, axis=0).T
    cols_ref[0] = even_cols
    cols_ref[1] = odd_cols
    for j in range(half):
        own = own_ref[j]
        other = other_ref[j]
        eff_even = jnp.where(odd, other[:, 2 * width :], own[:, 2 * width :])
        eff_odd = jnp.where(odd, own[:, 2 * width :], other[:, 2 * width :])
        even_total = jnp.where(odd, other[:, : 2 * width], own[:, : 2 * width])
        both = dot_ff(eff_odd, even_total)
        eff_ref[j, :count] = eff_even
        eff_ref[j, count:] = both[:, :width]
        read_ref[j, :count] = jnp.zeros((count, width), f32)
        read_ref[j, count:] = odd_cols[:, j : j + 1] * both[:, width:]


def quad_kernel(sel_ref, own_ref, other_ref, out_ref):
    width = own_ref.shape[1]
    upper = sel_ref[1] == 1
    for j in range(own_ref.shape[0]):
        own = own_ref[j]
        other = other_ref[j]
        out_ref[j] = composed(jnp.where(upper, own, other), jnp.where(upper, other, own), width)


def second_read_kernel(sel_ref, eff_ref, read_ref, cols_ref, low_ref, high_ref, eff_out, read_out):
    half, _, width = eff_ref.shape
    count = cols_ref.shape[1]
    heads = 2 * half
    share = low_ref.shape[0]
    upper = sel_ref[1] == 1
    for j in range(half):
        total = low_ref[j] if j < share else high_ref[j - share]
        eff = eff_ref[j]
        both = dot_ff(eff, total)
        eff_out[j] = jnp.where(upper, both[:, :width], eff)
        gain = jnp.concatenate([cols_ref[0, :, heads + j : heads + j + 1], cols_ref[1, :, heads + j : heads + j + 1]], axis=0)
        read_out[j] = read_ref[j] + jnp.where(upper, gain * both[:, width:], 0.0)


def climb_kernel(first, sel_ref, total_ref, prefix_ref, other_ref, memory_ref, total_out, prefix_out):
    width = total_ref.shape[1]
    upper = sel_ref[2] == 1
    for j in range(total_ref.shape[0]):
        own = total_ref[j]
        other = other_ref[j]
        if first:
            reached = other
        else:
            prefix = prefix_ref[j]
            reached = dot_ff(prefix, other)
        memory_ref[j] = jnp.where(upper, reached[:, width:], 0.0)
        if first:
            diagonal = lax.broadcasted_iota(jnp.int32, (width, width), 0) == lax.broadcasted_iota(jnp.int32, (width, width), 1)
            prefix = jnp.where(diagonal, 1.0, 0.0)
        prefix_out[j] = jnp.where(upper, reached[:, :width], prefix)
        total_out[j] = composed(jnp.where(upper, own, other), jnp.where(upper, other, own), width)


def top_kernel(sel_ref, prefix_ref, other_ref, memory_ref):
    upper = sel_ref[2] == 1
    for j in range(prefix_ref.shape[0]):
        memory_ref[j] = jnp.where(upper, dot_ff(prefix_ref[j], other_ref[j]), 0.0)


def level_read(level, upper, eff_ref, read_ref, cols_ref, own_ref, other_ref):
    half = eff_ref.shape[0]
    heads = 2 * half
    share = own_ref.shape[0]
    for j in range(half):
        own = own_ref[j % share]
        other = other_ref[j % share]
        memory = jnp.where(upper, other, own) if j < share else jnp.where(upper, own, other)
        at = level * heads + j
        gain = jnp.concatenate([cols_ref[0, :, at : at + 1], cols_ref[1, :, at : at + 1]], axis=0)
        yield j, read_ref[j] + gain * dot_ff(eff_ref[j], memory)


def read_kernel(level, sel_ref, eff_ref, read_ref, cols_ref, own_ref, other_ref, read_out):
    for j, total in level_read(level, sel_ref[1] == 1, eff_ref, read_ref, cols_ref, own_ref, other_ref):
        read_out[j] = total


def last_read_kernel(level, sel_ref, eff_ref, read_ref, cols_ref, own_ref, other_ref, keep_ref, send_ref):
    count = cols_ref.shape[1]
    width = eff_ref.shape[2]
    odd = sel_ref[0] == 1
    for j, total in level_read(level, sel_ref[1] == 1, eff_ref, read_ref, cols_ref, own_ref, other_ref):
        lanes = slice(j * width, (j + 1) * width)
        keep_ref[:, lanes] = jnp.where(odd, total[count:], total[:count])
        send_ref[:, lanes] = jnp.where(odd, total[:count], total[count:])


def join_kernel(sel_ref, keep_ref, got_ref, local_own_ref, local_other_ref, out_ref):
    span = keep_ref.shape[1]
    odd = sel_ref[0] == 1
    own = keep_ref[...] + local_own_ref[...]
    other = got_ref[...] + local_other_ref[...]
    out_ref[:, :span] = jnp.where(odd, other, own)
    out_ref[:, span:] = jnp.where(odd, own, other)


def run(kernel, out_shapes, sel, *arrays, name):
    return pl.pallas_call(
        kernel,
        out_shape=out_shapes,
        in_specs=[pl.BlockSpec(memory_space=pltpu.SMEM)]
        + [pl.BlockSpec(memory_space=pltpu.VMEM)] * len(arrays),
        name=name,
    )(sel, *arrays)


def array(*shape):
    return jax.ShapeDtypeStruct(shape, f32)


def block_half(which, half, queries, key_rows, value_rows, write_strength, log_decay, level_gates):
    count = queries.shape[0]
    width = queries.shape[1] // (2 * half)
    value_width = value_rows.shape[1] // (2 * half)
    wide = pl.BlockSpec((count, half * width), lambda i, which_ref: (0, which_ref[0]))
    whole = lambda value: pl.BlockSpec(value.shape, lambda i, which_ref: (0,) * value.ndim)
    return pl.pallas_call(
        block_kernel,
        grid_spec=pltpu.PrefetchScalarGridSpec(
            num_scalar_prefetch=1,
            grid=(1,),
            in_specs=[wide, wide, wide, whole(write_strength), whole(log_decay), whole(level_gates)],
            out_specs=[
                pl.BlockSpec((half, count, 2 * width + value_width), lambda i, which_ref: (0, 0, 0)),
                pl.BlockSpec((count, half * value_width), lambda i, which_ref: (0, 0)),
            ],
        ),
        out_shape=[array(half, count, 2 * width + value_width), array(count, half * value_width)],
        name="block",
    )(which, queries, key_rows, value_rows, write_strength, log_decay, level_gates)


def shards(queries, key_rows, value_rows, write_strength, log_decay, level_gates):
    size = lax.axis_size("ctx")
    levels = size.bit_length() - 1
    position = lax.axis_index("ctx")
    heads = write_strength.shape[0]
    half, share = heads // 2, heads // 4
    count = queries.shape[0]
    width = queries.shape[1] // heads
    core = position & 1
    row = (position >> 1) & 1
    inputs = (queries, key_rows, value_rows, write_strength, log_decay, level_gates)

    def swapped(value, bit):
        return lax.ppermute(value, "ctx", [(i, i ^ (1 << bit)) for i in range(size)])

    def choice(bit):
        return jnp.stack([core, row, (position >> bit) & 1]).astype(jnp.int32)

    sel = choice(2)
    gates_other = swapped(level_gates, 0)
    send, local_other = block_half((1 - core).reshape(1), half, *inputs)
    got = swapped(send, 0)
    own, local_own = block_half(core.reshape(1), half, *inputs)
    pair_send, pair_keep = run(
        pair_kernel, [array(share, width, 2 * width)] * 2, sel, own, got, name="pair"
    )
    pair_got = swapped(pair_send, 1)
    eff, read, cols = run(
        first_read_kernel,
        [array(half, 2 * count, width), array(half, 2 * count, width), array(2, count, count)],
        sel, own, got, level_gates, gates_other, name="read0",
    )
    total = run(quad_kernel, array(share, width, 2 * width), sel, pair_keep, pair_got, name="quad")
    low = lax.ppermute(
        pair_keep, "ctx", [(i, i + 2) for i in range(size) if (i >> 1) & 1 == 0]
    )
    prefix = None
    for level in range(2, levels):
        sel_level = choice(level)
        if level < levels - 1:
            other = swapped(total, level)
            first = prefix is None
            if first:
                prefix = jnp.zeros((share, width, width), f32)
            memory, total, prefix = run(
                lambda *refs, first=first: climb_kernel(first, *refs),
                [array(share, width, width), array(share, width, 2 * width), array(share, width, width)],
                sel_level, total, prefix, other, name="climb",
            )
        else:
            distance = 1 << level
            other = lax.ppermute(
                total[:, :, width:], "ctx", [(i, i + distance) for i in range(size - distance)]
            )
            memory = run(top_kernel, array(share, width, width), sel_level, prefix, other, name="top")
        memory_other = swapped(memory, 1)
        if level == 2:
            eff, read = run(
                second_read_kernel,
                [array(half, 2 * count, width), array(half, 2 * count, width)],
                sel, eff, read, cols, low, pair_got, name="read1",
            )
        if level < levels - 1:
            read = run(
                lambda *refs, level=level: read_kernel(level, *refs),
                array(half, 2 * count, width),
                sel, eff, read, cols, memory, memory_other, name="readn",
            )
        else:
            keep, away = run(
                lambda *refs, level=level: last_read_kernel(level, *refs),
                [array(count, half * width)] * 2,
                sel, eff, read, cols, memory, memory_other, name="readlast",
            )
    back = swapped(away, 0)
    return run(
        join_kernel, array(count, heads * width), sel, keep, back, local_own, local_other, name="join"
    )


def solution(mesh):
    placed = (
        P(("groups", "ctx"), None),
        P(("groups", "ctx"), None),
        P(("groups", "ctx"), None),
        P(None, ("groups", "ctx")),
        P(None, ("groups", "ctx")),
        P(None, None, ("groups", "ctx")),
    )
    return jax.shard_map(
        shards, mesh=mesh, in_specs=placed, out_specs=P(("groups", "ctx"), None), check_vma=False
    )
```

```python
import jax
import jax.numpy as jnp
from jax import lax
from jax.experimental import pallas as pl
from jax.experimental.pallas import tpu as pltpu
from jax.sharding import PartitionSpec as P

norm_eps = 1e-06
f32 = jnp.float32
bf16 = jnp.bfloat16


def parts(value):
    high = value.astype(bf16)
    return high, (value - high.astype(f32)).astype(bf16)


def mm(left, right, dims=((1,), (0,))):
    return lax.dot_general(left, right, (dims, ((), ())), preferred_element_type=f32)


def dot_ff(left, right):
    width = right.shape[1]
    left_parts = jnp.concatenate(parts(left), axis=1)
    right_row = jnp.concatenate(parts(right), axis=1)
    both = mm(left_parts, jnp.concatenate([right_row, right_row], axis=0))
    return both[:, :width] + both[:, width:]


def dot_fb(left, right):
    left_parts = jnp.concatenate(parts(left), axis=1)
    return mm(left_parts, jnp.concatenate([right, right], axis=0))


def dot_bf_t(left, right):
    width = right.shape[1]
    both = mm(left, jnp.concatenate(parts(right), axis=1), ((0,), (0,)))
    return both[:, :width] + both[:, width:]


def bit_of(pos_ref, bit):
    return ((pos_ref[0] >> bit) & 1) == 1


def block_kernel(mine, pos_ref, q_ref, k_ref, v_ref, beta_ref, decay_ref, gates_ref, planes_ref, local_ref):
    heads = beta_ref.shape[0]
    half = heads // 2
    count = q_ref.shape[0]
    width = q_ref.shape[1] // half
    upper = bit_of(pos_ref, 0) if mine else jnp.logical_not(bit_of(pos_ref, 0))

    def chosen_first(rows):
        return jnp.where(upper, pltpu.roll(rows, half, 0), rows)

    row = lax.broadcasted_iota(jnp.int32, (count, count), 0)
    col = lax.broadcasted_iota(jnp.int32, (count, count), 1)
    summing = jnp.where(row <= col, 1.0, 0.0).astype(bf16)
    decay = decay_ref[...]
    d1 = decay.astype(bf16)
    rest = decay - d1.astype(f32)
    d2 = rest.astype(bf16)
    d3 = (rest - d2.astype(f32)).astype(bf16)
    running = chosen_first(mm(d1, summing) + (mm(d2, summing) + mm(d3, summing)))
    beta = chosen_first(beta_ref[...])
    growth = jnp.exp(running)
    to_end = jnp.exp(running[:, count - 1 :] - running)
    kinds = [running, beta, growth, to_end] + [chosen_first(gates_ref[b]) for b in range(gates_ref.shape[0])]
    filler = jnp.zeros((count - len(kinds) * heads, count), f32)
    columns = jnp.concatenate(kinds + [filler], axis=0).T
    planes_ref[3 * half] = columns

    def column(kind, head):
        return columns[:, kind * heads + head : kind * heads + head + 1]

    k_rows, q_rows, k_norm = [], [], jnp.zeros((count, count), f32)
    scales = []
    for j in range(half):
        lanes = slice(j * width, (j + 1) * width)
        kj = k_ref[:, lanes]
        qj = q_ref[:, lanes]
        kf = kj.astype(f32)
        qf = qj.astype(f32)
        k_scale = lax.rsqrt(jnp.sum(kf * kf, axis=1, keepdims=True) + norm_eps)
        q_scale = lax.rsqrt(jnp.sum(qf * qf, axis=1, keepdims=True) + norm_eps)
        k_norm = jnp.where(col == j, k_scale, k_norm)
        k_rows.append(kj)
        q_rows.append(qj)
        scales.append((k_scale, q_scale))
    k_norm_rows = k_norm.T

    lower_incl = row >= col
    belows, inverses, query_grams = [], [], []
    for j in range(half):
        k_scale, q_scale = scales[j]
        kj = k_rows[j]
        gap = jnp.where(lower_incl, column(0, j) - running[j : j + 1], 0.0)
        ratio = jnp.where(lower_incl, jnp.exp(gap), 0.0) * k_norm_rows[j : j + 1]
        grams = mm(jnp.concatenate([kj, q_rows[j]], axis=0), kj, ((1,), (1,)))
        below = grams[:count] * ratio * (column(1, j) * k_scale)
        query_grams.append(grams[count:] * ratio * q_scale)
        belows.append(below)
        first = jnp.where((row ^ col) == 1, below, 0.0)
        inverses.append(jnp.where(row == col, 1.0, jnp.where(row > col, -first, 0.0)))
    level = 1
    while (1 << level) < count:
        pair = ((row >> level) ^ (col >> level)) == 1
        pair = pair & (row > col)
        for j in range(half):
            link = jnp.where(pair, belows[j], 0.0)
            inverse = inverses[j]
            inverses[j] = inverse - dot_ff(inverse, dot_ff(link, inverse))
        level += 1
    for j in range(half):
        lanes = slice(j * width, (j + 1) * width)
        k_scale, q_scale = scales[j]
        kj = k_rows[j]
        inverse = inverses[j]
        from_query = dot_ff(query_grams[j], inverse)
        from_key = dot_bf_t(kj, inverse * (column(3, j) * k_scale))
        both = jnp.concatenate([from_query, from_key], axis=0)
        beta_row = beta[j : j + 1]
        written = dot_fb(both * beta_row, v_ref[:, lanes])
        erased = dot_fb(both * (beta_row * growth[j : j + 1] * k_norm_rows[j : j + 1]), kj)
        local_ref[:, lanes] = column(4, j) * written[:count]
        last = growth[j : j + 1, count - 1 :]
        planes_ref[3 * j] = jnp.where(row == col, last, 0.0) - erased[count:]
        planes_ref[3 * j + 1] = written[count:]
        planes_ref[3 * j + 2] = (column(2, j) * q_scale) * q_rows[j].astype(f32) - erased[:count]


def composed(later_trans, later_state, earlier):
    width = later_state.shape[1]
    both = dot_ff(later_trans, earlier)
    return jnp.concatenate([both[:, :width], both[:, width:] + later_state], axis=1)


def group_step(upper, own, other):
    width = own.shape[0]
    later = jnp.where(upper, own, other)
    return composed(later[:, :width], later[:, width:], jnp.where(upper, other, own))


def block_total(planes_ref, head):
    return jnp.concatenate([planes_ref[3 * head], planes_ref[3 * head + 1]], axis=1)


def pair_kernel(pos_ref, own_ref, other_ref, send_ref, keep_ref):
    share = send_ref.shape[0]
    odd = bit_of(pos_ref, 0)
    x = (pos_ref[0] >> 1) & 1
    for target, base in ((send_ref, (1 - x) * share), (keep_ref, x * share)):
        for j in range(share):
            own = block_total(own_ref, base + j)
            other = block_total(other_ref, base + j)
            target[j] = group_step(odd, own, other)


def gate_column(pos_ref, own_ref, other_ref, kind):
    at = own_ref.shape[0] - 1
    odd = bit_of(pos_ref, 0)
    own = own_ref[at, :, kind : kind + 1]
    other = other_ref[at, :, kind : kind + 1]
    return jnp.where(odd, other, own), jnp.where(odd, own, other)


def first_read_kernel(heads, pos_ref, own_ref, other_ref, eff_ref, read_ref):
    half = heads // 2
    count, width = own_ref.shape[1:]
    odd = bit_of(pos_ref, 0)
    for j in range(half):
        own_eff = own_ref[3 * j + 2]
        other_eff = other_ref[3 * j + 2]
        earlier = jnp.where(odd, block_total(other_ref, j), block_total(own_ref, j))
        both = dot_ff(jnp.where(odd, own_eff, other_eff), earlier)
        gain = gate_column(pos_ref, own_ref, other_ref, 5 * heads + j)[1]
        eff_ref[j, :count] = jnp.where(odd, other_eff, own_eff)
        eff_ref[j, count:] = both[:, :width]
        read_ref[j, :count] = jnp.zeros((count, width), f32)
        read_ref[j, count:] = gain * both[:, width:]


def quad_kernel(pos_ref, own_ref, other_ref, out_ref):
    upper = bit_of(pos_ref, 1)
    for j in range(own_ref.shape[0]):
        out_ref[j] = group_step(upper, own_ref[j], other_ref[j])


def second_read_kernel(heads, pos_ref, eff_ref, read_ref, low_ref, high_ref, own_ref, other_ref, eff_out, read_out):
    half = heads // 2
    width = eff_ref.shape[2]
    share = low_ref.shape[0]
    upper = bit_of(pos_ref, 1)
    for j in range(half):
        total = low_ref[j] if j < share else high_ref[j - share]
        eff = eff_ref[j]
        both = dot_ff(eff, total)
        eff_out[j] = jnp.where(upper, both[:, :width], eff)
        gain = jnp.concatenate(gate_column(pos_ref, own_ref, other_ref, 6 * heads + j), axis=0)
        read_out[j] = read_ref[j] + jnp.where(upper, gain * both[:, width:], 0.0)


def climb_kernel(level, first, top_next, pos_ref, total_ref, other_ref, *refs):
    prefix_ref = None if first else refs[0]
    memory_ref, prefix_out, total_out = refs[-3:]
    width = total_ref.shape[1]
    upper = bit_of(pos_ref, level)
    row = lax.broadcasted_iota(jnp.int32, (width, width), 0)
    col = lax.broadcasted_iota(jnp.int32, (width, width), 1)
    for j in range(total_ref.shape[0]):
        own = total_ref[j]
        other = other_ref[j]
        if first:
            prefix = jnp.where(row == col, 1.0, 0.0)
            reached = other
        else:
            prefix = prefix_ref[j]
            reached = dot_ff(prefix, other)
        memory_ref[j] = jnp.where(upper, reached[:, width:], 0.0)
        prefix_out[j] = jnp.where(upper, reached[:, :width], prefix)
        if top_next:
            later = jnp.where(upper, own, other)
            earlier = jnp.where(upper, other[:, width:], own[:, width:])
            total_out[j] = dot_ff(later[:, :width], earlier) + later[:, width:]
        else:
            total_out[j] = group_step(upper, own, other)


def top_kernel(level, pos_ref, prefix_ref, other_ref, memory_ref):
    upper = bit_of(pos_ref, level)
    for j in range(prefix_ref.shape[0]):
        memory_ref[j] = jnp.where(upper, dot_ff(prefix_ref[j], other_ref[j]), 0.0)


def level_memory(pos_ref, mine_ref, others_ref, head):
    share = mine_ref.shape[0]
    upper = bit_of(pos_ref, 1)
    mine = mine_ref[head % share]
    others = others_ref[head % share]
    return jnp.where(upper, others, mine) if head < share else jnp.where(upper, mine, others)


def read_kernel(heads, level, pos_ref, eff_ref, read_ref, mine_ref, others_ref, own_ref, other_ref, read_out):
    for j in range(heads // 2):
        gain = jnp.concatenate(
            gate_column(pos_ref, own_ref, other_ref, (5 + level) * heads + j), axis=0
        )
        memory = level_memory(pos_ref, mine_ref, others_ref, j)
        read_out[j] = read_ref[j] + gain * dot_ff(eff_ref[j], memory)


def last_read_kernel(heads, level, pos_ref, eff_ref, read_ref, mine_ref, others_ref, own_ref, other_ref, keep_ref, send_ref):
    count = own_ref.shape[1]
    width = eff_ref.shape[2]
    odd = bit_of(pos_ref, 0)
    for j in range(heads // 2):
        gain = jnp.concatenate(
            gate_column(pos_ref, own_ref, other_ref, (5 + level) * heads + j), axis=0
        )
        memory = level_memory(pos_ref, mine_ref, others_ref, j)
        total = read_ref[j] + gain * dot_ff(eff_ref[j], memory)
        lanes = slice(j * width, (j + 1) * width)
        keep_ref[:, lanes] = jnp.where(odd, total[count:], total[:count])
        send_ref[:, lanes] = jnp.where(odd, total[:count], total[count:])


def join_kernel(pos_ref, keep_ref, got_ref, local_own_ref, local_other_ref, out_ref):
    span = keep_ref.shape[1]
    odd = bit_of(pos_ref, 0)
    own = keep_ref[...] + local_own_ref[...]
    other = got_ref[...] + local_other_ref[...]
    out_ref[:, :span] = jnp.where(odd, other, own)
    out_ref[:, span:] = jnp.where(odd, own, other)


def near(*shape):
    return pltpu.VMEM(shape, f32)


def far(*shape):
    return jax.ShapeDtypeStruct(shape, f32)


def params():
    return pltpu.CompilerParams(vmem_limit_bytes=16 << 20)


def run(kernel, out_shapes, position, *arrays, name):
    held = [pltpu.with_memory_space_constraint(value, pltpu.VMEM) for value in arrays]
    return pl.pallas_call(
        kernel,
        out_shape=out_shapes,
        in_specs=[pl.BlockSpec(memory_space=pltpu.SMEM)]
        + [pl.BlockSpec(memory_space=pltpu.VMEM)] * len(arrays),
        compiler_params=params(),
        name=name,
    )(position, *held)


def block_half(mine, position, queries, key_rows, value_rows, write_strength, log_decay, level_gates):
    count = queries.shape[0]
    half = write_strength.shape[0] // 2
    span = value_rows.shape[1] // 2

    def side(i, pos_ref):
        core = pos_ref[0] & 1
        return (0, core if mine else 1 - core)

    wide = pl.BlockSpec((count, span), side)
    whole = lambda value: pl.BlockSpec(value.shape, lambda i, pos_ref: (0,) * value.ndim)
    return pl.pallas_call(
        lambda *refs: block_kernel(mine, *refs),
        grid_spec=pltpu.PrefetchScalarGridSpec(
            num_scalar_prefetch=1,
            grid=(1,),
            in_specs=[wide, wide, wide, whole(write_strength), whole(log_decay), whole(level_gates)],
            out_specs=[pl.BlockSpec(memory_space=pltpu.VMEM)] * 2,
        ),
        out_shape=[near(3 * half + 1, count, count), near(count, span)],
        compiler_params=params(),
        name="block_own" if mine else "block_sent",
    )(position, queries, key_rows, value_rows, write_strength, log_decay, level_gates)


def shards(queries, key_rows, value_rows, write_strength, log_decay, level_gates):
    size = lax.axis_size("ctx")
    levels = size.bit_length() - 1
    position = lax.axis_index("ctx").astype(jnp.int32).reshape(1)
    heads = write_strength.shape[0]
    half, share = heads // 2, heads // 4
    count = queries.shape[0]
    width = queries.shape[1] // heads
    inputs = (queries, key_rows, value_rows, write_strength, log_decay, level_gates)

    def swapped(value, bit):
        return lax.ppermute(value, "ctx", [(i, i ^ (1 << bit)) for i in range(size)])

    sent, local_other = block_half(False, position, *inputs)
    got = swapped(sent, 0)
    own, local_own = block_half(True, position, *inputs)
    pair_send, pair_keep = run(
        pair_kernel, [near(share, width, 2 * width)] * 2, position, own, got, name="pair"
    )
    pair_got = swapped(pair_send, 1)
    eff, read = run(
        lambda *refs: first_read_kernel(heads, *refs),
        [near(half, 2 * count, width)] * 2,
        position, own, got, name="read_first",
    )
    pair_got, eff, read = lax.optimization_barrier((pair_got, eff, read))
    total = run(quad_kernel, near(share, width, 2 * width), position, pair_keep, pair_got, name="quad")
    low = lax.ppermute(
        pair_keep, "ctx", [(i, i + 2) for i in range(size) if (i >> 1) & 1 == 0]
    )
    prefix, pending = (), []
    for level in range(2, levels - 1):
        other = swapped(total, level)
        memory, prefix, total = run(
            lambda *refs, level=level, first=not prefix: climb_kernel(
                level, first, level == levels - 2, *refs
            ),
            [near(share, width, width)] * 2
            + [near(share, width, width if level == levels - 2 else 2 * width)],
            position, total, other, *prefix, name="climb",
        )
        prefix = (prefix,)
        pending.append((level, memory, swapped(memory, 1)))
    top = levels - 1
    other = lax.ppermute(total, "ctx", [(i, i + (1 << top)) for i in range(size - (1 << top))])
    eff, read = run(
        lambda *refs: second_read_kernel(heads, *refs),
        [near(half, 2 * count, width)] * 2,
        position, eff, read, low, pair_got, own, got, name="read_second",
    )
    for level, memory, memory_other in pending:
        read = run(
            lambda *refs, level=level: read_kernel(heads, level, *refs),
            near(half, 2 * count, width),
            position, eff, read, memory, memory_other, own, got, name="read_level",
        )
    other, eff, read = lax.optimization_barrier((other, eff, read))
    memory = run(
        lambda *refs: top_kernel(top, *refs), near(share, width, width), position, *prefix, other, name="top"
    )
    memory_other = swapped(memory, 1)
    keep, away = run(
        lambda *refs: last_read_kernel(heads, top, *refs),
        [near(count, half * width)] * 2,
        position, eff, read, memory, memory_other, own, got, name="read_last",
    )
    back = swapped(away, 0)
    return run(
        join_kernel, far(count, heads * width), position, keep, back, local_own, local_other, name="join"
    )


def solution(mesh):
    placed = (
        P(("groups", "ctx"), None),
        P(("groups", "ctx"), None),
        P(("groups", "ctx"), None),
        P(None, ("groups", "ctx")),
        P(None, ("groups", "ctx")),
        P(None, None, ("groups", "ctx")),
    )
    return jax.shard_map(
        shards, mesh=mesh, in_specs=placed, out_specs=P(("groups", "ctx"), None), check_vma=False
    )
```

```python
import functools

import jax
import jax.numpy as jnp
from jax import lax
from jax.experimental import pallas as pl
from jax.experimental.pallas import tpu as pltpu
from jax.sharding import PartitionSpec as P

norm_eps = 1e-06
f32 = jnp.float32
bf16 = jnp.bfloat16


def parts(value):
    high = value.astype(bf16)
    return high, (value - high.astype(f32)).astype(bf16)


def mm(left, right, dims=((1,), (0,))):
    return lax.dot_general(left, right, (dims, ((), ())), preferred_element_type=f32)


def dot_ff(left, right):
    width = right.shape[1]
    left_parts = jnp.concatenate(parts(left), axis=1)
    right_row = jnp.concatenate(parts(right), axis=1)
    both = mm(left_parts, jnp.concatenate([right_row, right_row], axis=0))
    return both[:, :width] + both[:, width:]


def dot_fb(left, right):
    left_parts = jnp.concatenate(parts(left), axis=1)
    return mm(left_parts, jnp.concatenate([right, right], axis=0))


def dot_bf_t(left, right):
    width = right.shape[1]
    both = mm(left, jnp.concatenate(parts(right), axis=1), ((0,), (0,)))
    return both[:, :width] + both[:, width:]


chunks = 2


def bit_of(pos_ref, bit):
    return ((pos_ref[0] >> bit) & 1) == 1


def prepare_kernel(pos_ref, *refs):
    arrays = refs[:6]
    q_ref, k_ref, v_ref, rows_ref, columns_ref, beta_ref, decay_ref, gates_ref, sems = refs[6:]
    targets = (q_ref, k_ref, v_ref, beta_ref, decay_ref, gates_ref)
    copies = [pltpu.make_async_copy(a, t, sems.at[i]) for i, (a, t) in enumerate(zip(arrays, targets))]
    for i in (4, 3, 5, 1, 0, 2):
        copies[i].start()
    heads, count = beta_ref.shape
    half = heads // 2
    odd = bit_of(pos_ref, 0)

    def chosen_first(rows):
        return jnp.where(odd, pltpu.roll(rows, half, 0), rows)

    row = lax.broadcasted_iota(jnp.int32, (count, count), 0)
    col = lax.broadcasted_iota(jnp.int32, (count, count), 1)
    summing = jnp.where(row <= col, 1.0, 0.0).astype(bf16)
    for i in (4, 3, 5):
        copies[i].wait()
    decay = decay_ref[...]
    d1 = decay.astype(bf16)
    rest = decay - d1.astype(f32)
    d2 = rest.astype(bf16)
    d3 = (rest - d2.astype(f32)).astype(bf16)
    running = chosen_first(mm(d1, summing) + (mm(d2, summing) + mm(d3, summing)))
    beta = chosen_first(beta_ref[...])
    growth = jnp.exp(running)
    to_end = jnp.exp(running[:, count - 1 :] - running)
    kinds = [running, beta, growth, to_end] + [chosen_first(gates_ref[b]) for b in range(gates_ref.shape[0])]
    filler = jnp.zeros((count - len(kinds) * heads, count), f32)
    columns_ref[...] = jnp.concatenate(kinds + [filler], axis=0).T
    rows_ref[...] = jnp.concatenate(kinds[:3], axis=0)
    for i in (1, 0, 2):
        copies[i].wait()


def block_kernel(heads, mine, pos_ref, q_ref, k_ref, v_ref, rows_ref, columns_ref, planes_ref, local_ref):
    half = heads // 2
    n = half
    count = q_ref.shape[0]
    width = q_ref.shape[1] // heads
    core = pos_ref[0] & 1
    side = core if mine else 1 - core
    row = lax.broadcasted_iota(jnp.int32, (count, count), 0)
    col = lax.broadcasted_iota(jnp.int32, (count, count), 1)
    base = 0 if mine else half
    columns = columns_ref[...]
    if planes_ref.shape[0] > 3 * n:
        planes_ref[3 * n] = columns

    def column(kind, j):
        at = kind * heads + base + j
        return columns[:, at : at + 1]

    def line(kind, j):
        at = kind * heads + base + j
        return rows_ref[at : at + 1]

    def lanes(ref, j):
        at = pl.multiple_of(side * (half * width) + j * width, 128)
        return ref[:, pl.ds(at, width)]

    k_rows, q_rows, k_norm = [], [], jnp.zeros((count, count), f32)
    scales = []
    for j in range(n):
        kj = lanes(k_ref, j)
        qj = lanes(q_ref, j)
        kf = kj.astype(f32)
        qf = qj.astype(f32)
        k_scale = lax.rsqrt(jnp.sum(kf * kf, axis=1, keepdims=True) + norm_eps)
        q_scale = lax.rsqrt(jnp.sum(qf * qf, axis=1, keepdims=True) + norm_eps)
        k_norm = jnp.where(col == j, k_scale, k_norm)
        k_rows.append(kj)
        q_rows.append(qj)
        scales.append((k_scale, q_scale))
    k_norm_rows = k_norm.T

    lower_incl = row >= col
    belows, query_grams, runs = [], [], []
    for j in range(n):
        k_scale, q_scale = scales[j]
        kj = k_rows[j]
        run_row = line(0, j)
        run_all = jnp.broadcast_to(column(0, j), (count, count))
        runs.append(run_all)
        gap = jnp.where(lower_incl, run_all - run_row, 0.0)
        ratio = jnp.where(lower_incl, jnp.exp(gap), 0.0) * k_norm_rows[j : j + 1]
        grams = mm(jnp.concatenate([kj, q_rows[j]], axis=0), kj, ((1,), (1,)))
        below = jnp.where(row > col, grams[:count] * ratio * (column(1, j) * k_scale), 0.0)
        query_grams.append(grams[count:] * ratio * q_scale)
        belows.append(below)
    step = 16
    folded = jnp.concatenate([folded_blocks(belows[j], step, row, col) for j in range(n)], axis=0)
    own_col = lax.broadcasted_iota(jnp.int32, (step, count), 1) % step
    own_row = lax.broadcasted_iota(jnp.int32, (step, count), 0)
    group = lax.broadcasted_iota(jnp.int32, folded.shape, 1) // step * step
    solved = [jnp.where(own_col == own_row, 1.0, 0.0)] * n
    for s in range(step - 1):
        factors = jnp.take_along_axis(folded, group + s, axis=1)
        for j in range(n):
            solved[j] = solved[j] - factors[j * step : (j + 1) * step] * solved[j][s : s + 1]
    inverses = []
    for j in range(n):
        spread = jnp.concatenate([solved[j]] * (count // step), axis=0)
        inverses.append(jnp.where(row // step == col // step, spread, 0.0))
    while step < count:
        pair = ((row // step) % 2 == 1) & (row // (2 * step) == col // (2 * step)) & ((col // step) % 2 == 0)
        starts = range(0, count, 2 * step)
        for j in range(n):
            inverse = inverses[j]
            odd_rows = jnp.concatenate([inverse[i + step : i + 2 * step] for i in starts], axis=0)
            link = jnp.where(pair, belows[j], 0.0)
            odd_rows = odd_rows - dot_ff(dot_ff(odd_rows, link), inverse)
            both = []
            for at, i in enumerate(starts):
                both += [inverse[i : i + step], odd_rows[at * step : (at + 1) * step]]
            inverses[j] = jnp.concatenate(both, axis=0)
        step *= 2
    for j in range(n):
        k_scale, q_scale = scales[j]
        kj = k_rows[j]
        inverse = inverses[j]
        run_end = line(0, j)[:, count - 1 :]
        from_query = dot_ff(query_grams[j], inverse)
        from_key = dot_bf_t(kj, inverse * (jnp.exp(run_end - runs[j]) * k_scale))
        both = jnp.concatenate([from_query, from_key], axis=0)
        beta_row = line(1, j)
        growth = line(2, j)
        written = dot_fb(both * beta_row, lanes(v_ref, j))
        erased = dot_fb(both * (beta_row * growth * k_norm_rows[j : j + 1]), kj)
        local_ref[:, j * width : (j + 1) * width] = written[:count]
        planes_ref[3 * j] = jnp.where(row == col, growth[:, count - 1 :], 0.0) - erased[count:]
        planes_ref[3 * j + 1] = written[count:]
        planes_ref[3 * j + 2] = (jnp.exp(runs[j]) * q_scale) * q_rows[j].astype(f32) - erased[:count]


def folded_blocks(matrix, step, row, col):
    count = matrix.shape[0]
    kept = jnp.where(row // step == col // step, matrix, 0.0)
    total = kept[:step]
    for i in range(step, count, step):
        total = total + kept[i : i + step]
    return total


def group_step(upper, own, other):
    width = own.shape[0]
    later = jnp.where(upper, own, other)
    both = dot_ff(later[:, :width], jnp.where(upper, other, own))
    return jnp.concatenate([both[:, :width], both[:, width:] + later[:, width:]], axis=1)


def block_total(planes_ref, head):
    return jnp.concatenate([planes_ref[3 * head], planes_ref[3 * head + 1]], axis=1)


def pair_kernel(pos_ref, own_ref, other_ref, *refs):
    share = refs[0].shape[0]
    width = own_ref.shape[1]
    odd = bit_of(pos_ref, 0)
    x = (pos_ref[0] >> 1) & 1
    low_ref = refs[-1]
    for c in range(chunks):
        for target, base in ((refs[2 * c], (1 - x) * share), (refs[2 * c + 1], x * share)):
            for j in range(share):
                at = base + c * 2 * share + j
                total = group_step(odd, block_total(own_ref, at), block_total(other_ref, at))
                target[j] = total
                if target is refs[2 * c + 1]:
                    low_ref[c + j * chunks] = total[:, width:]


def gate_columns(heads, level, j, pos_ref, own_ref, other_ref):
    half = heads // 2
    odd = bit_of(pos_ref, 0)
    at = (4 + level) * heads + j
    own = own_ref[:, at : at + 1]
    other = other_ref[other_ref.shape[0] - 1, :, at + half : at + half + 1]
    return jnp.where(odd, other, own), jnp.where(odd, own, other)


def first_read_kernel(heads, pos_ref, own_ref, other_ref, cols_ref, local_ref, local_sent_ref, eff_ref, read_ref, out_ref, sent_out):
    count, width = own_ref.shape[1:]
    half = heads // 2
    odd = bit_of(pos_ref, 0)
    for j in range(half):
        own_eff = own_ref[3 * j + 2]
        other_eff = other_ref[3 * j + 2]
        earlier = jnp.where(odd, block_total(other_ref, j), block_total(own_ref, j))
        both = dot_ff(jnp.where(odd, own_eff, other_eff), earlier)
        gain = gate_columns(heads, 1, j, pos_ref, cols_ref, other_ref)[1]
        eff_ref[j, :count] = jnp.where(odd, other_eff, own_eff)
        eff_ref[j, count:] = both[:, :width]
        read_ref[j, :count] = jnp.zeros((count, width), f32)
        read_ref[j, count:] = gain * both[:, width:]
        lanes = slice(j * width, (j + 1) * width)
        at = 4 * heads + j
        out_ref[:, lanes] = cols_ref[:, at : at + 1] * local_ref[:, lanes]
        sent_out[:, lanes] = cols_ref[:, at + half : at + half + 1] * local_sent_ref[:, lanes]


def quad_kernel(pos_ref, own_ref, other_ref, out_ref):
    upper = bit_of(pos_ref, 1)
    for j in range(own_ref.shape[0]):
        out_ref[j] = group_step(upper, own_ref[j], other_ref[j])


def climb_kernel(level, top_next, pieces, pos_ref, *refs):
    first = level == 2
    use_ref, send_ref, prefix_out, total_out = refs[-4:]
    width = use_ref.shape[1]
    upper = bit_of(pos_ref, level)
    x = bit_of(pos_ref, 1)
    row = lax.broadcasted_iota(jnp.int32, (width, width), 0)
    col = lax.broadcasted_iota(jnp.int32, (width, width), 1)
    for at in range(use_ref.shape[0]):
        c, j = at % pieces, at // pieces
        total_ref, other_ref = refs[c], refs[pieces + c]
        own = total_ref[j]
        other = other_ref[j]
        later = jnp.where(upper, own, other)
        if top_next:
            earlier = jnp.where(upper, other[:, width:], own[:, width:])
            total_out[at] = dot_ff(later[:, :width], earlier) + later[:, width:]
        else:
            total_out[at] = group_step(upper, own, other)
        if first:
            keep_ref, got_ref = refs[2 * pieces + c], refs[3 * pieces + c]
            passed = jnp.where(x, got_ref[j, :, :width], keep_ref[j, :, :width])
            prefix = jnp.concatenate([jnp.where(row == col, 1.0, 0.0), passed], axis=0)
            reached = jnp.concatenate([other, dot_ff(passed, other)], axis=0)
        else:
            prefix = refs[2 * pieces][at]
            reached = dot_ff(prefix, other)
        prefix_out[at] = jnp.where(upper, reached[:, :width], prefix)
        memory = jnp.where(upper, reached[:, width:], 0.0)
        use_ref[at] = jnp.where(x, memory[width:], memory[:width])
        send_ref[at] = jnp.where(x, memory[:width], memory[width:])


def top_kernel(level, pos_ref, prefix_ref, other_ref, use_ref, send_ref):
    width = other_ref.shape[1]
    upper = bit_of(pos_ref, level)
    x = bit_of(pos_ref, 1)
    for j in range(prefix_ref.shape[0]):
        memory = jnp.where(upper, dot_ff(prefix_ref[j], other_ref[j]), 0.0)
        use_ref[j] = jnp.where(x, memory[width:], memory[:width])
        send_ref[j] = jnp.where(x, memory[:width], memory[width:])


def gain_of(heads, level, j, pos_ref, cols_ref, got_ref):
    return jnp.concatenate(gate_columns(heads, level + 1, j, pos_ref, cols_ref, got_ref), axis=0)


def owned(x, j, share, mine, others):
    return jnp.where(x, others, mine) if j < share else jnp.where(x, mine, others)


def read_kernel(heads, level, top, pos_ref, eff_ref, read_ref, cols_ref, planes_ref, use_ref, got_ref, *refs):
    share, width = use_ref.shape[:2]
    low_refs, outs = (refs[: chunks + 1], refs[chunks + 1 :]) if level == 2 else ((), refs)
    x = bit_of(pos_ref, 1)
    for head in range(heads // 2):
        c, j = divmod(head, 2 * share // chunks)
        at = c + j % (share // chunks) * chunks
        memory = owned(x, j, share // chunks, use_ref[at], got_ref[at])
        gain = gain_of(heads, level, head, pos_ref, cols_ref, planes_ref)
        eff = eff_ref[head]
        if level > 2:
            outs[0][head] = read_ref[head] + gain * dot_ff(eff, memory)
        else:
            low_ref, pair_ref = low_refs[0], low_refs[1 + c]
            below = low_ref[at] if j < share // chunks else pair_ref[j - share // chunks, :, width:]
            both = dot_ff(eff, jnp.concatenate([jnp.where(x, below, 0.0), memory], axis=1))
            first = gain_of(heads, 1, head, pos_ref, cols_ref, planes_ref)
            outs[0][head] = read_ref[head] + first * both[:, :width] + gain * both[:, width:]
        if level == top - 1:
            outs[1][head] = gain_of(heads, top, head, pos_ref, cols_ref, planes_ref) * eff


def last_read_kernel(pos_ref, eff_ref, read_ref, use_ref, got_ref, keep_ref, away_ref):
    share, width = use_ref.shape[:2]
    count = keep_ref.shape[0]
    odd = bit_of(pos_ref, 0)
    x = bit_of(pos_ref, 1)
    for head in range(2 * share):
        c, j = divmod(head, 2 * share // chunks)
        at = c + j % (share // chunks) * chunks
        memory = owned(x, j, share // chunks, use_ref[at], got_ref[at])
        total = read_ref[head] + dot_ff(eff_ref[head], memory)
        lanes = slice(head * width, (head + 1) * width)
        keep_ref[:, lanes] = jnp.where(odd, total[count:], total[:count])
        away_ref[:, lanes] = jnp.where(odd, total[:count], total[count:])


def join_kernel(pos_ref, own_ref, sent_ref, keep_ref, got_ref, out_ref):
    half = out_ref.shape[1] // 2
    odd = bit_of(pos_ref, 0)
    own = keep_ref[...] + own_ref[...]
    other = got_ref[...] + sent_ref[...]
    out_ref[:, :half] = jnp.where(odd, other, own)
    out_ref[:, half:] = jnp.where(odd, own, other)


def near(*shape):
    return pltpu.VMEM(shape, f32)


def params():
    return pltpu.CompilerParams(vmem_limit_bytes=16 << 20)


def run(kernel, out_shapes, position, *arrays, name, static=()):
    held = [pltpu.with_memory_space_constraint(value, pltpu.VMEM) for value in arrays]
    return pl.pallas_call(
        lambda *refs: kernel(*static, *refs),
        out_shape=out_shapes,
        in_specs=[pl.BlockSpec(memory_space=pltpu.SMEM)]
        + [pl.BlockSpec(memory_space=pltpu.VMEM)] * len(arrays),
        compiler_params=params(),
        name=name,
    )(position, *held)


def prepare(position, queries, key_rows, value_rows, write_strength, log_decay, level_gates):
    heads = write_strength.shape[0]
    count = queries.shape[0]
    arrays = (queries, key_rows, value_rows, write_strength, log_decay, level_gates)
    return pl.pallas_call(
        prepare_kernel,
        out_shape=[pltpu.VMEM(value.shape, value.dtype) for value in arrays[:3]]
        + [near(3 * heads, count), near(count, count)],
        in_specs=[pl.BlockSpec(memory_space=pltpu.SMEM)] + [pl.BlockSpec(memory_space=pl.ANY)] * 6,
        scratch_shapes=[pltpu.VMEM(value.shape, value.dtype) for value in arrays[3:]]
        + [pltpu.SemaphoreType.DMA((6,))],
        compiler_params=params(),
        name="prepare",
    )(position, *[pltpu.with_memory_space_constraint(value, pltpu.HBM) for value in arrays])


def shards(queries, key_rows, value_rows, write_strength, log_decay, level_gates):
    size = lax.axis_size("ctx")
    levels = size.bit_length() - 1
    top = levels - 1
    position = lax.axis_index("ctx").astype(jnp.int32).reshape(1)
    heads = write_strength.shape[0]
    half = heads // 2
    share = half // chunks // 2
    count = queries.shape[0]
    width = queries.shape[1] // heads

    def swapped(value, bit):
        return lax.ppermute(value, "ctx", [(i, i ^ (1 << bit)) for i in range(size)])

    *tokens, columns = prepare(
        position, queries, key_rows, value_rows, write_strength, log_decay, level_gates
    )
    sent, local_sent = run(
        block_kernel, [near(3 * half + 1, count, count), near(count, half * width)],
        position, *tokens, columns, name="block_sent", static=(heads, False),
    )
    got = swapped(sent, 0)
    own, local_own = run(
        block_kernel, [near(3 * half, count, count), near(count, half * width)],
        position, *tokens, columns, name="block_own", static=(heads, True),
    )
    *pairs, low = run(
        pair_kernel,
        [near(share, width, 2 * width)] * (2 * chunks) + [near(chunks * share, width, width)],
        position, own, got, name="pair",
    )
    pairs_got = [swapped(pairs[2 * c], 1) for c in range(chunks)]
    eff, read, local_own, local_sent = run(
        first_read_kernel,
        [near(half, 2 * count, width)] * 2 + [near(count, half * width)] * 2,
        position, own, got, columns, local_own, local_sent, name="read_first", static=(heads,),
    )
    pairs_got[0], eff, read, local_own, local_sent = lax.optimization_barrier(
        (pairs_got[0], eff, read, local_own, local_sent)
    )
    totals = [
        run(quad_kernel, near(share, width, 2 * width), position, pairs[2 * c + 1], pairs_got[c], name="quad")
        for c in range(chunks)
    ]
    low, _ = lax.optimization_barrier((low, pairs_got[-1]))
    low = lax.ppermute(low, "ctx", [(i, i + 2) for i in range(size) if (i >> 1) & 1 == 0])
    owned_heads = chunks * share
    prefix = (*pairs[1::2], *pairs_got)
    pending = []
    for level in range(2, top):
        top_next = level == top - 1
        others = [swapped(total, level) for total in totals]
        use, send, *prefix, total = run(
            climb_kernel,
            [near(owned_heads, width, width)] * 2
            + [near(owned_heads, 2 * width, width), near(owned_heads, width, width if top_next else 2 * width)],
            position, *totals, *others, *prefix, name="climb", static=(level, top_next, len(totals)),
        )
        totals = [total]
        pending.append((level, use, send))
    distance = 1 << top
    other = lax.ppermute(totals[0], "ctx", [(i, i + distance) for i in range(size - distance)])
    for level, use, send in pending:
        extra = (low, *pairs_got) if level == 2 else ()
        read, *gated = run(
            functools.partial(read_kernel, heads, level, top),
            [near(half, 2 * count, width)] * (2 if level == top - 1 else 1), position, eff, read, columns,
            got, use, swapped(send, 1), *extra, name="read",
        )
    other, read = lax.optimization_barrier((other, read))
    use, send = run(
        top_kernel, [near(owned_heads, width, width)] * 2, position, *prefix, other, name="top", static=(top,)
    )
    keep, away = run(
        last_read_kernel, [near(count, half * width)] * 2,
        position, *gated, read, use, swapped(send, 1), name="read_last",
    )
    return run(
        join_kernel, jax.ShapeDtypeStruct((count, heads * width), f32), position, local_own, local_sent,
        keep, swapped(away, 0), name="join",
    )


def solution(mesh):
    placed = (
        P(("groups", "ctx"), None),
        P(("groups", "ctx"), None),
        P(("groups", "ctx"), None),
        P(None, ("groups", "ctx")),
        P(None, ("groups", "ctx")),
        P(None, None, ("groups", "ctx")),
    )
    return jax.shard_map(
        shards, mesh=mesh, in_specs=placed, out_specs=P(("groups", "ctx"), None), check_vma=False
    )
```

```python
import functools

import jax
import jax.numpy as jnp
from jax import lax
from jax.experimental import pallas as pl
from jax.experimental.pallas import tpu as pltpu
from jax.sharding import PartitionSpec as P

norm_eps = 1e-06
f32 = jnp.float32
bf16 = jnp.bfloat16


def parts(value):
    high = value.astype(bf16)
    return high, (value - high.astype(f32)).astype(bf16)


def mm(left, right, dims=((1,), (0,))):
    return lax.dot_general(left, right, (dims, ((), ())), preferred_element_type=f32)


def dot_ff(left, right):
    width = right.shape[1]
    left_parts = jnp.concatenate(parts(left), axis=1)
    right_row = jnp.concatenate(parts(right), axis=1)
    both = mm(left_parts, jnp.concatenate([right_row, right_row], axis=0))
    return both[:, :width] + both[:, width:]


def dot_fb(left, right):
    left_parts = jnp.concatenate(parts(left), axis=1)
    return mm(left_parts, jnp.concatenate([right, right], axis=0))


def dot_bf_t(left, right):
    width = right.shape[1]
    both = mm(left, jnp.concatenate(parts(right), axis=1), ((0,), (0,)))
    return both[:, :width] + both[:, width:]


chunks = 2


def bit_of(pos_ref, bit):
    return ((pos_ref[0] >> bit) & 1) == 1


def prepare_kernel(pos_ref, *refs):
    arrays = refs[:6]
    q_ref, k_ref, v_ref, rows_ref, columns_ref, beta_ref, decay_ref, gates_ref, sems = refs[6:]
    targets = (q_ref, k_ref, v_ref, beta_ref, decay_ref, gates_ref)
    copies = [pltpu.make_async_copy(a, t, sems.at[i]) for i, (a, t) in enumerate(zip(arrays, targets))]
    for i in (4, 3, 5, 1, 0, 2):
        copies[i].start()
    heads, count = beta_ref.shape
    half = heads // 2
    odd = bit_of(pos_ref, 0)

    def chosen_first(rows):
        return jnp.where(odd, pltpu.roll(rows, half, 0), rows)

    row = lax.broadcasted_iota(jnp.int32, (count, count), 0)
    col = lax.broadcasted_iota(jnp.int32, (count, count), 1)
    summing = jnp.where(row <= col, 1.0, 0.0).astype(bf16)
    for i in (4, 3, 5):
        copies[i].wait()
    decay = decay_ref[...]
    d1 = decay.astype(bf16)
    rest = decay - d1.astype(f32)
    d2 = rest.astype(bf16)
    d3 = (rest - d2.astype(f32)).astype(bf16)
    running = chosen_first(mm(d1, summing) + (mm(d2, summing) + mm(d3, summing)))
    beta = chosen_first(beta_ref[...])
    growth = jnp.exp(running)
    to_end = jnp.exp(running[:, count - 1 :] - running)
    kinds = [running, beta, growth, to_end] + [chosen_first(gates_ref[b]) for b in range(gates_ref.shape[0])]
    filler = jnp.zeros((count - len(kinds) * heads, count), f32)
    columns_ref[...] = jnp.concatenate(kinds + [filler], axis=0).T
    rows_ref[...] = jnp.concatenate(kinds[:3], axis=0)
    for i in (1, 0, 2):
        copies[i].wait()


def block_kernel(heads, mine, pos_ref, q_ref, k_ref, v_ref, rows_ref, columns_ref, planes_ref, local_ref):
    half = heads // 2
    n = half
    count = q_ref.shape[0]
    width = q_ref.shape[1] // heads
    core = pos_ref[0] & 1
    side = core if mine else 1 - core
    row = lax.broadcasted_iota(jnp.int32, (count, count), 0)
    col = lax.broadcasted_iota(jnp.int32, (count, count), 1)
    base = 0 if mine else half
    columns = columns_ref[...]
    if planes_ref.shape[0] > 3 * n:
        planes_ref[3 * n] = columns

    def column(kind, j):
        at = kind * heads + base + j
        return columns[:, at : at + 1]

    def line(kind, j):
        at = kind * heads + base + j
        return rows_ref[at : at + 1]

    def lanes(ref, j):
        at = pl.multiple_of(side * (half * width) + j * width, 128)
        return ref[:, pl.ds(at, width)]

    k_rows, q_rows, k_norm = [], [], jnp.zeros((count, count), f32)
    scales = []
    for j in range(n):
        kj = lanes(k_ref, j)
        qj = lanes(q_ref, j)
        kf = kj.astype(f32)
        qf = qj.astype(f32)
        k_scale = lax.rsqrt(jnp.sum(kf * kf, axis=1, keepdims=True) + norm_eps)
        q_scale = lax.rsqrt(jnp.sum(qf * qf, axis=1, keepdims=True) + norm_eps)
        k_norm = jnp.where(col == j, k_scale, k_norm)
        k_rows.append(kj)
        q_rows.append(qj)
        scales.append((k_scale, q_scale))
    k_norm_rows = k_norm.T

    lower_incl = row >= col
    belows, query_grams, runs = [], [], []
    for j in range(n):
        k_scale, q_scale = scales[j]
        kj = k_rows[j]
        run_row = line(0, j)
        run_all = jnp.broadcast_to(column(0, j), (count, count))
        runs.append(run_all)
        gap = jnp.where(lower_incl, run_all - run_row, 0.0)
        ratio = jnp.where(lower_incl, jnp.exp(gap), 0.0) * k_norm_rows[j : j + 1]
        grams = mm(jnp.concatenate([kj, q_rows[j]], axis=0), kj, ((1,), (1,)))
        below = jnp.where(row > col, grams[:count] * ratio * (column(1, j) * k_scale), 0.0)
        query_grams.append(grams[count:] * ratio * q_scale)
        belows.append(below)
    step = 16
    folded = jnp.concatenate([folded_blocks(belows[j], step, row, col) for j in range(n)], axis=0)
    own_col = lax.broadcasted_iota(jnp.int32, (step, count), 1) % step
    own_row = lax.broadcasted_iota(jnp.int32, (step, count), 0)
    group = lax.broadcasted_iota(jnp.int32, folded.shape, 1) // step * step
    solved = [jnp.where(own_col == own_row, 1.0, 0.0)] * n
    for s in range(step - 1):
        factors = jnp.take_along_axis(folded, group + s, axis=1)
        for j in range(n):
            solved[j] = solved[j] - factors[j * step : (j + 1) * step] * solved[j][s : s + 1]
    inverses = []
    for j in range(n):
        spread = jnp.concatenate([solved[j]] * (count // step), axis=0)
        inverses.append(jnp.where(row // step == col // step, spread, 0.0))
    while step < count:
        pair = ((row // step) % 2 == 1) & (row // (2 * step) == col // (2 * step)) & ((col // step) % 2 == 0)
        starts = range(0, count, 2 * step)
        for j in range(n):
            inverse = inverses[j]
            odd_rows = jnp.concatenate([inverse[i + step : i + 2 * step] for i in starts], axis=0)
            link = jnp.where(pair, belows[j], 0.0)
            odd_rows = odd_rows - dot_ff(dot_ff(odd_rows, link), inverse)
            both = []
            for at, i in enumerate(starts):
                both += [inverse[i : i + step], odd_rows[at * step : (at + 1) * step]]
            inverses[j] = jnp.concatenate(both, axis=0)
        step *= 2
    for j in range(n):
        k_scale, q_scale = scales[j]
        kj = k_rows[j]
        inverse = inverses[j]
        run_end = line(0, j)[:, count - 1 :]
        from_query = dot_ff(query_grams[j], inverse)
        from_key = dot_bf_t(kj, inverse * (jnp.exp(run_end - runs[j]) * k_scale))
        both = jnp.concatenate([from_query, from_key], axis=0)
        beta_row = line(1, j)
        growth = line(2, j)
        written = dot_fb(both * beta_row, lanes(v_ref, j))
        erased = dot_fb(both * (beta_row * growth * k_norm_rows[j : j + 1]), kj)
        local_ref[:, j * width : (j + 1) * width] = written[:count]
        planes_ref[3 * j] = jnp.where(row == col, growth[:, count - 1 :], 0.0) - erased[count:]
        planes_ref[3 * j + 1] = written[count:]
        planes_ref[3 * j + 2] = (jnp.exp(runs[j]) * q_scale) * q_rows[j].astype(f32) - erased[:count]


def folded_blocks(matrix, step, row, col):
    count = matrix.shape[0]
    kept = jnp.where(row // step == col // step, matrix, 0.0)
    total = kept[:step]
    for i in range(step, count, step):
        total = total + kept[i : i + step]
    return total


def group_step(upper, own, other):
    width = own.shape[0]
    later = jnp.where(upper, own, other)
    both = dot_ff(later[:, :width], jnp.where(upper, other, own))
    return jnp.concatenate([both[:, :width], both[:, width:] + later[:, width:]], axis=1)


def block_total(planes_ref, head):
    return jnp.concatenate([planes_ref[3 * head], planes_ref[3 * head + 1]], axis=1)


def pair_kernel(pos_ref, own_ref, other_ref, *refs):
    share = refs[0].shape[0]
    width = own_ref.shape[1]
    odd = bit_of(pos_ref, 0)
    x = (pos_ref[0] >> 1) & 1
    low_ref = refs[-1]
    for c in range(chunks):
        for target, base in ((refs[2 * c], (1 - x) * share), (refs[2 * c + 1], x * share)):
            for j in range(share):
                at = base + c * 2 * share + j
                total = group_step(odd, block_total(own_ref, at), block_total(other_ref, at))
                target[j] = total
                if target is refs[2 * c + 1]:
                    low_ref[c + j * chunks] = total[:, width:]


def gate_columns(heads, level, j, pos_ref, own_ref, other_ref):
    half = heads // 2
    odd = bit_of(pos_ref, 0)
    at = (4 + level) * heads + j
    own = own_ref[:, at : at + 1]
    other = other_ref[other_ref.shape[0] - 1, :, at + half : at + half + 1]
    return jnp.where(odd, other, own), jnp.where(odd, own, other)


def first_read_kernel(heads, pos_ref, own_ref, other_ref, cols_ref, local_ref, local_sent_ref, eff_ref, read_ref, out_ref, sent_out):
    count, width = own_ref.shape[1:]
    half = heads // 2
    odd = bit_of(pos_ref, 0)
    for j in range(half):
        own_eff = own_ref[3 * j + 2]
        other_eff = other_ref[3 * j + 2]
        earlier = jnp.where(odd, block_total(other_ref, j), block_total(own_ref, j))
        both = dot_ff(jnp.where(odd, own_eff, other_eff), earlier)
        gain = gate_columns(heads, 1, j, pos_ref, cols_ref, other_ref)[1]
        eff_ref[j, :count] = jnp.where(odd, other_eff, own_eff)
        eff_ref[j, count:] = both[:, :width]
        read_ref[j, :count] = jnp.zeros((count, width), f32)
        read_ref[j, count:] = gain * both[:, width:]
        lanes = slice(j * width, (j + 1) * width)
        at = 4 * heads + j
        out_ref[:, lanes] = cols_ref[:, at : at + 1] * local_ref[:, lanes]
        sent_out[:, lanes] = cols_ref[:, at + half : at + half + 1] * local_sent_ref[:, lanes]


def quad_kernel(pos_ref, own_ref, other_ref, out_ref):
    upper = bit_of(pos_ref, 1)
    for j in range(own_ref.shape[0]):
        out_ref[j] = group_step(upper, own_ref[j], other_ref[j])


def climb_kernel(level, top_next, pieces, pos_ref, *refs):
    first = level == 2
    use_ref, send_ref, prefix_out, total_out = refs[-4:]
    width = use_ref.shape[1]
    upper = bit_of(pos_ref, level)
    x = bit_of(pos_ref, 1)
    row = lax.broadcasted_iota(jnp.int32, (width, width), 0)
    col = lax.broadcasted_iota(jnp.int32, (width, width), 1)
    for at in range(use_ref.shape[0]):
        c, j = at % pieces, at // pieces
        total_ref, other_ref = refs[c], refs[pieces + c]
        own = total_ref[j]
        other = other_ref[j]
        later = jnp.where(upper, own, other)
        if top_next:
            earlier = jnp.where(upper, other[:, width:], own[:, width:])
            total_out[at] = dot_ff(later[:, :width], earlier) + later[:, width:]
        else:
            total_out[at] = group_step(upper, own, other)
        if first:
            keep_ref, got_ref = refs[2 * pieces + c], refs[3 * pieces + c]
            passed = jnp.where(x, got_ref[j, :, :width], keep_ref[j, :, :width])
            prefix = jnp.concatenate([jnp.where(row == col, 1.0, 0.0), passed], axis=0)
            reached = jnp.concatenate([other, dot_ff(passed, other)], axis=0)
        else:
            prefix = refs[2 * pieces][at]
            reached = dot_ff(prefix, other)
        prefix_out[at] = jnp.where(upper, reached[:, :width], prefix)
        memory = jnp.where(upper, reached[:, width:], 0.0)
        use_ref[at] = jnp.where(x, memory[width:], memory[:width])
        send_ref[at] = jnp.where(x, memory[:width], memory[width:])


def top_kernel(level, pos_ref, prefix_ref, other_ref, use_ref, send_ref):
    width = other_ref.shape[1]
    upper = bit_of(pos_ref, level)
    x = bit_of(pos_ref, 1)
    for j in range(prefix_ref.shape[0]):
        memory = jnp.where(upper, dot_ff(prefix_ref[j], other_ref[j]), 0.0)
        use_ref[j] = jnp.where(x, memory[width:], memory[:width])
        send_ref[j] = jnp.where(x, memory[:width], memory[width:])


def gain_of(heads, level, j, pos_ref, cols_ref, got_ref):
    return jnp.concatenate(gate_columns(heads, level + 1, j, pos_ref, cols_ref, got_ref), axis=0)


def owned(x, j, share, mine, others):
    return jnp.where(x, others, mine) if j < share else jnp.where(x, mine, others)


def read_kernel(heads, level, top, pos_ref, eff_ref, read_ref, cols_ref, planes_ref, use_ref, got_ref, *refs):
    share, width = use_ref.shape[:2]
    low_refs, outs = (refs[: chunks + 1], refs[chunks + 1 :]) if level == 2 else ((), refs)
    x = bit_of(pos_ref, 1)
    for head in range(heads // 2):
        c, j = divmod(head, 2 * share // chunks)
        at = c + j % (share // chunks) * chunks
        memory = owned(x, j, share // chunks, use_ref[at], got_ref[at])
        gain = gain_of(heads, level, head, pos_ref, cols_ref, planes_ref)
        eff = eff_ref[head]
        if level > 2:
            outs[0][head] = read_ref[head] + gain * dot_ff(eff, memory)
        else:
            low_ref, pair_ref = low_refs[0], low_refs[1 + c]
            below = low_ref[at] if j < share // chunks else pair_ref[j - share // chunks, :, width:]
            both = dot_ff(eff, jnp.concatenate([jnp.where(x, below, 0.0), memory], axis=1))
            first = gain_of(heads, 1, head, pos_ref, cols_ref, planes_ref)
            outs[0][head] = read_ref[head] + first * both[:, :width] + gain * both[:, width:]
        if level == top - 1:
            outs[1][head] = gain_of(heads, top, head, pos_ref, cols_ref, planes_ref) * eff


def last_read_kernel(pos_ref, eff_ref, read_ref, use_ref, got_ref, keep_ref, away_ref):
    share, width = use_ref.shape[:2]
    count = keep_ref.shape[0]
    odd = bit_of(pos_ref, 0)
    x = bit_of(pos_ref, 1)
    for head in range(2 * share):
        c, j = divmod(head, 2 * share // chunks)
        at = c + j % (share // chunks) * chunks
        memory = owned(x, j, share // chunks, use_ref[at], got_ref[at])
        total = read_ref[head] + dot_ff(eff_ref[head], memory)
        lanes = slice(head * width, (head + 1) * width)
        keep_ref[:, lanes] = jnp.where(odd, total[count:], total[:count])
        away_ref[:, lanes] = jnp.where(odd, total[:count], total[count:])


def join_kernel(pos_ref, own_ref, sent_ref, keep_ref, got_ref, out_ref):
    half = out_ref.shape[1] // 2
    odd = bit_of(pos_ref, 0)
    own = keep_ref[...] + own_ref[...]
    other = got_ref[...] + sent_ref[...]
    out_ref[:, :half] = jnp.where(odd, other, own)
    out_ref[:, half:] = jnp.where(odd, own, other)


def near(*shape):
    return pltpu.VMEM(shape, f32)


def params():
    return pltpu.CompilerParams(vmem_limit_bytes=16 << 20)


def run(kernel, out_shapes, position, *arrays, name, static=()):
    held = [pltpu.with_memory_space_constraint(value, pltpu.VMEM) for value in arrays]
    return pl.pallas_call(
        lambda *refs: kernel(*static, *refs),
        out_shape=out_shapes,
        in_specs=[pl.BlockSpec(memory_space=pltpu.SMEM)]
        + [pl.BlockSpec(memory_space=pltpu.VMEM)] * len(arrays),
        compiler_params=params(),
        name=name,
    )(position, *held)


def prepare(position, queries, key_rows, value_rows, write_strength, log_decay, level_gates):
    heads = write_strength.shape[0]
    count = queries.shape[0]
    arrays = (queries, key_rows, value_rows, write_strength, log_decay, level_gates)
    return pl.pallas_call(
        prepare_kernel,
        out_shape=[pltpu.VMEM(value.shape, value.dtype) for value in arrays[:3]]
        + [near(3 * heads, count), near(count, count)],
        in_specs=[pl.BlockSpec(memory_space=pltpu.SMEM)] + [pl.BlockSpec(memory_space=pl.ANY)] * 6,
        scratch_shapes=[pltpu.VMEM(value.shape, value.dtype) for value in arrays[3:]]
        + [pltpu.SemaphoreType.DMA((6,))],
        compiler_params=params(),
        name="prepare",
    )(position, *[pltpu.with_memory_space_constraint(value, pltpu.HBM) for value in arrays])


def shards(queries, key_rows, value_rows, write_strength, log_decay, level_gates):
    size = lax.axis_size("ctx")
    levels = size.bit_length() - 1
    top = levels - 1
    position = lax.axis_index("ctx").astype(jnp.int32).reshape(1)
    heads = write_strength.shape[0]
    half = heads // 2
    share = half // chunks // 2
    count = queries.shape[0]
    width = queries.shape[1] // heads

    def swapped(value, bit):
        return lax.ppermute(value, "ctx", [(i, i ^ (1 << bit)) for i in range(size)])

    *tokens, columns = prepare(
        position, queries, key_rows, value_rows, write_strength, log_decay, level_gates
    )
    sent, local_sent = run(
        block_kernel, [near(3 * half + 1, count, count), near(count, half * width)],
        position, *tokens, columns, name="block_sent", static=(heads, False),
    )
    got = swapped(sent, 0)
    own, local_own = run(
        block_kernel, [near(3 * half, count, count), near(count, half * width)],
        position, *tokens, columns, name="block_own", static=(heads, True),
    )
    *pairs, low = run(
        pair_kernel,
        [near(share, width, 2 * width)] * (2 * chunks) + [near(chunks * share, width, width)],
        position, own, got, name="pair",
    )
    pairs_got = [swapped(pairs[2 * c], 1) for c in range(chunks)]
    eff, read, local_own, local_sent = run(
        first_read_kernel,
        [near(half, 2 * count, width)] * 2 + [near(count, half * width)] * 2,
        position, own, got, columns, local_own, local_sent, name="read_first", static=(heads,),
    )
    pairs_got[0], eff, read, local_own, local_sent = lax.optimization_barrier(
        (pairs_got[0], eff, read, local_own, local_sent)
    )
    totals = [
        run(quad_kernel, near(share, width, 2 * width), position, pairs[2 * c + 1], pairs_got[c], name="quad")
        for c in range(chunks)
    ]
    low, _ = lax.optimization_barrier((low, pairs_got[-1]))
    low = swapped(low, 1)
    owned_heads = chunks * share
    prefix = (*pairs[1::2], *pairs_got)
    pending = []
    for level in range(2, top):
        top_next = level == top - 1
        others = [swapped(total, level) for total in totals]
        use, send, *prefix, total = run(
            climb_kernel,
            [near(owned_heads, width, width)] * 2
            + [near(owned_heads, 2 * width, width), near(owned_heads, width, width if top_next else 2 * width)],
            position, *totals, *others, *prefix, name="climb", static=(level, top_next, len(totals)),
        )
        totals = [total]
        pending.append((level, use, send))
    other = swapped(totals[0], top)
    use, send = run(
        top_kernel, [near(owned_heads, width, width)] * 2, position, *prefix, other, name="top", static=(top,)
    )
    last_other = swapped(send, 1)
    for level, level_use, level_send in pending:
        extra = (low, *pairs_got) if level == 2 else ()
        level_other = swapped(level_send, 1)
        if level == top - 1:
            level_other, _ = lax.optimization_barrier((level_other, send))
        read, *gated = run(
            functools.partial(read_kernel, heads, level, top),
            [near(half, 2 * count, width)] * (2 if level == top - 1 else 1), position, eff, read, columns,
            got, level_use, level_other, *extra, name="read",
        )
    keep, away = run(
        last_read_kernel, [near(count, half * width)] * 2,
        position, *gated, read, use, last_other, name="read_last",
    )
    return run(
        join_kernel, jax.ShapeDtypeStruct((count, heads * width), f32), position, local_own, local_sent,
        keep, swapped(away, 0), name="join",
    )


def solution(mesh):
    placed = (
        P(("groups", "ctx"), None),
        P(("groups", "ctx"), None),
        P(("groups", "ctx"), None),
        P(None, ("groups", "ctx")),
        P(None, ("groups", "ctx")),
        P(None, None, ("groups", "ctx")),
    )
    return jax.shard_map(
        shards, mesh=mesh, in_specs=placed, out_specs=P(("groups", "ctx"), None), check_vma=False
    )
```

```python
import functools

import jax
import jax.numpy as jnp
from jax import lax
from jax.experimental import pallas as pl
from jax.experimental.pallas import tpu as pltpu
from jax.sharding import PartitionSpec as P

norm_eps = 1e-06
f32 = jnp.float32
bf16 = jnp.bfloat16


def parts(value):
    high = value.astype(bf16)
    return high, (value - high.astype(f32)).astype(bf16)


def mm(left, right, dims=((1,), (0,))):
    return lax.dot_general(left, right, (dims, ((), ())), preferred_element_type=f32)


def dot_ff(left, right):
    width = right.shape[1]
    left_parts = jnp.concatenate(parts(left), axis=1)
    right_row = jnp.concatenate(parts(right), axis=1)
    both = mm(left_parts, jnp.concatenate([right_row, right_row], axis=0))
    return both[:, :width] + both[:, width:]


def dot_fb(left, right):
    left_parts = jnp.concatenate(parts(left), axis=1)
    return mm(left_parts, jnp.concatenate([right, right], axis=0))


def dot_bf_t(left, right):
    width = right.shape[1]
    both = mm(left, jnp.concatenate(parts(right), axis=1), ((0,), (0,)))
    return both[:, :width] + both[:, width:]


chunks = 2


def bit_of(pos_ref, bit):
    return ((pos_ref[0] >> bit) & 1) == 1


def opening_kernel(pos_ref, *refs):
    arrays = refs[:6]
    q_ref, k_ref, v_ref, rows_ref, columns_ref, planes_ref, inverse_ref = refs[6:13]
    beta_ref, decay_ref, gates_ref, sems = refs[13:]
    targets = (q_ref, k_ref, v_ref, beta_ref, decay_ref, gates_ref)
    copies = [pltpu.make_async_copy(a, t, sems.at[i]) for i, (a, t) in enumerate(zip(arrays, targets))]
    for i in (4, 3, 5, 1, 2, 0):
        copies[i].start()
    heads, count = beta_ref.shape
    half = heads // 2
    odd = bit_of(pos_ref, 0)

    def chosen_first(rows):
        return jnp.where(odd, pltpu.roll(rows, half, 0), rows)

    row = lax.broadcasted_iota(jnp.int32, (count, count), 0)
    col = lax.broadcasted_iota(jnp.int32, (count, count), 1)
    summing = jnp.where(row <= col, 1.0, 0.0).astype(bf16)
    for i in (4, 3, 5):
        copies[i].wait()
    decay = decay_ref[...]
    d1 = decay.astype(bf16)
    rest = decay - d1.astype(f32)
    d2 = rest.astype(bf16)
    d3 = (rest - d2.astype(f32)).astype(bf16)
    running = chosen_first(mm(d1, summing) + (mm(d2, summing) + mm(d3, summing)))
    beta = chosen_first(beta_ref[...])
    growth = jnp.exp(running)
    to_end = jnp.exp(running[:, count - 1 :] - running)
    kinds = [running, beta, growth, to_end] + [chosen_first(gates_ref[b]) for b in range(gates_ref.shape[0])]
    filler = jnp.zeros((count - len(kinds) * heads, count), f32)
    columns_ref[...] = jnp.concatenate(kinds + [filler], axis=0).T
    rows_ref[...] = jnp.concatenate(kinds[:3], axis=0)
    copies[1].wait()
    copies[2].wait()
    block_kernel(heads, False, pos_ref, k_ref, v_ref, rows_ref, columns_ref, planes_ref, inverse_ref)
    copies[0].wait()


class Tokens:
    def __init__(self, heads, mine, pos_ref, rows_ref, columns_ref):
        self.heads, self.half = heads, heads // 2
        core = pos_ref[0] & 1
        self.side = core if mine else 1 - core
        self.base = 0 if mine else self.half
        self.rows_ref, self.columns = rows_ref, columns_ref[...]
        count = self.columns.shape[0]
        self.row = lax.broadcasted_iota(jnp.int32, (count, count), 0)
        self.col = lax.broadcasted_iota(jnp.int32, (count, count), 1)
        self.lower_incl = self.row >= self.col

    def column(self, kind, j):
        at = kind * self.heads + self.base + j
        return self.columns[:, at : at + 1]

    def line(self, kind, j):
        at = kind * self.heads + self.base + j
        return self.rows_ref[at : at + 1]

    def lanes(self, ref, j):
        width = ref.shape[1] // self.heads
        at = pl.multiple_of(self.side * (self.half * width) + j * width, 128)
        return ref[:, pl.ds(at, width)]

    def scale(self, ref, j):
        value = self.lanes(ref, j).astype(f32)
        return lax.rsqrt(jnp.sum(value * value, axis=1, keepdims=True) + norm_eps)

    def scale_rows(self, scales):
        value = jnp.zeros(self.row.shape, f32)
        for j, scale in enumerate(scales):
            value = jnp.where(self.col == j, scale, value)
        return value.T

    def run_all(self, j):
        return jnp.broadcast_to(self.column(0, j), self.row.shape)

    def ratio(self, run_all, j):
        gap = jnp.where(self.lower_incl, run_all - self.line(0, j), 0.0)
        return jnp.where(self.lower_incl, jnp.exp(gap), 0.0)


def block_kernel(heads, mine, pos_ref, k_ref, v_ref, rows_ref, columns_ref, planes_ref, inverse_ref):
    t = Tokens(heads, mine, pos_ref, rows_ref, columns_ref)
    n, row, col = t.half, t.row, t.col
    count = row.shape[0]
    scales = [t.scale(k_ref, j) for j in range(n)]
    norm_rows = t.scale_rows(scales)
    belows, runs = [], []
    for j in range(n):
        kj = t.lanes(k_ref, j)
        runs.append(t.run_all(j))
        ratio = t.ratio(runs[j], j) * norm_rows[j : j + 1]
        gram = mm(kj, kj, ((1,), (1,)))
        belows.append(jnp.where(row > col, gram * ratio * (t.column(1, j) * scales[j]), 0.0))
    step = 16
    folded = jnp.concatenate([folded_blocks(belows[j], step, row, col) for j in range(n)], axis=0)
    own_col = lax.broadcasted_iota(jnp.int32, (step, count), 1) % step
    own_row = lax.broadcasted_iota(jnp.int32, (step, count), 0)
    group = lax.broadcasted_iota(jnp.int32, folded.shape, 1) // step * step
    solved = [jnp.where(own_col == own_row, 1.0, 0.0)] * n
    for s in range(step - 1):
        factors = jnp.take_along_axis(folded, group + s, axis=1)
        for j in range(n):
            solved[j] = solved[j] - factors[j * step : (j + 1) * step] * solved[j][s : s + 1]
    inverses = []
    for j in range(n):
        spread = jnp.concatenate([solved[j]] * (count // step), axis=0)
        inverses.append(jnp.where(row // step == col // step, spread, 0.0))
    while step < count:
        pair = ((row // step) % 2 == 1) & (row // (2 * step) == col // (2 * step)) & ((col // step) % 2 == 0)
        starts = range(0, count, 2 * step)
        for j in range(n):
            inverse = inverses[j]
            odd_rows = jnp.concatenate([inverse[i + step : i + 2 * step] for i in starts], axis=0)
            link = jnp.where(pair, belows[j], 0.0)
            odd_rows = odd_rows - dot_ff(dot_ff(odd_rows, link), inverse)
            both = []
            for at, i in enumerate(starts):
                both += [inverse[i : i + step], odd_rows[at * step : (at + 1) * step]]
            inverses[j] = jnp.concatenate(both, axis=0)
        step *= 2
    for j in range(n):
        kj = t.lanes(k_ref, j)
        inverse = inverses[j]
        inverse_ref[j] = inverse
        run_end = t.line(0, j)[:, count - 1 :]
        from_key = dot_bf_t(kj, inverse * (jnp.exp(run_end - runs[j]) * scales[j]))
        beta_row, growth = t.line(1, j), t.line(2, j)
        erased = dot_fb(from_key * (beta_row * growth * norm_rows[j : j + 1]), kj)
        planes_ref[2 * j] = jnp.where(row == col, growth[:, count - 1 :], 0.0) - erased
        planes_ref[2 * j + 1] = dot_fb(from_key * beta_row, t.lanes(v_ref, j))


def query_kernel(heads, mine, pos_ref, q_ref, k_ref, v_ref, rows_ref, columns_ref, inverse_ref, eff_ref, local_ref):
    t = Tokens(heads, mine, pos_ref, rows_ref, columns_ref)
    n = t.half
    width = q_ref.shape[1] // heads
    norm_rows = t.scale_rows([t.scale(k_ref, j) for j in range(n)])
    for j in range(n):
        kj = t.lanes(k_ref, j)
        qj = t.lanes(q_ref, j)
        q_scale = t.scale(q_ref, j)
        run_all = t.run_all(j)
        ratio = t.ratio(run_all, j) * norm_rows[j : j + 1]
        gram = mm(qj, kj, ((1,), (1,))) * ratio * q_scale
        from_query = dot_ff(gram, inverse_ref[j])
        beta_row, growth = t.line(1, j), t.line(2, j)
        written = dot_fb(from_query * beta_row, t.lanes(v_ref, j))
        erased = dot_fb(from_query * (beta_row * growth * norm_rows[j : j + 1]), kj)
        local_ref[:, j * width : (j + 1) * width] = t.column(4, j) * written
        eff_ref[j] = (jnp.exp(run_all) * q_scale) * qj.astype(f32) - erased
    if not mine:
        eff_ref[n] = t.columns


def folded_blocks(matrix, step, row, col):
    count = matrix.shape[0]
    kept = jnp.where(row // step == col // step, matrix, 0.0)
    total = kept[:step]
    for i in range(step, count, step):
        total = total + kept[i : i + step]
    return total


def group_step(upper, own, other):
    width = own.shape[0]
    later = jnp.where(upper, own, other)
    both = dot_ff(later[:, :width], jnp.where(upper, other, own))
    return jnp.concatenate([both[:, :width], both[:, width:] + later[:, width:]], axis=1)


def block_total(planes_ref, head):
    return jnp.concatenate([planes_ref[2 * head], planes_ref[2 * head + 1]], axis=1)


def pair_kernel(pos_ref, own_ref, other_ref, *refs):
    share = refs[0].shape[0]
    width = own_ref.shape[1]
    odd = bit_of(pos_ref, 0)
    x = (pos_ref[0] >> 1) & 1
    low_ref = refs[-1]
    for c in range(chunks):
        for target, base in ((refs[2 * c], (1 - x) * share), (refs[2 * c + 1], x * share)):
            for j in range(share):
                at = base + c * 2 * share + j
                total = group_step(odd, block_total(own_ref, at), block_total(other_ref, at))
                target[j] = total
                if target is refs[2 * c + 1]:
                    low_ref[c + j * chunks] = total[:, width:]


def gate_columns(heads, level, j, pos_ref, own_ref, other_ref):
    half = heads // 2
    odd = bit_of(pos_ref, 0)
    at = (4 + level) * heads + j
    own = own_ref[:, at : at + 1]
    other = other_ref[other_ref.shape[0] - 1, :, at + half : at + half + 1]
    return jnp.where(odd, other, own), jnp.where(odd, own, other)


def first_read_kernel(heads, pos_ref, own_ref, other_ref, own_eff_ref, other_eff_ref, cols_ref, eff_ref, read_ref):
    count, width = own_ref.shape[1:]
    odd = bit_of(pos_ref, 0)
    for j in range(heads // 2):
        own_eff = own_eff_ref[j]
        other_eff = other_eff_ref[j]
        earlier = jnp.where(odd, block_total(other_ref, j), block_total(own_ref, j))
        both = dot_ff(jnp.where(odd, own_eff, other_eff), earlier)
        gain = gate_columns(heads, 1, j, pos_ref, cols_ref, other_eff_ref)[1]
        eff_ref[j, :count] = jnp.where(odd, other_eff, own_eff)
        eff_ref[j, count:] = both[:, :width]
        read_ref[j, :count] = jnp.zeros((count, width), f32)
        read_ref[j, count:] = gain * both[:, width:]


def quad_kernel(pos_ref, own_ref, other_ref, out_ref):
    upper = bit_of(pos_ref, 1)
    for j in range(own_ref.shape[0]):
        out_ref[j] = group_step(upper, own_ref[j], other_ref[j])


def climb_kernel(level, top_next, pieces, pos_ref, *refs):
    first = level == 2
    use_ref, send_ref, prefix_out, total_out = refs[-4:]
    width = use_ref.shape[1]
    upper = bit_of(pos_ref, level)
    x = bit_of(pos_ref, 1)
    row = lax.broadcasted_iota(jnp.int32, (width, width), 0)
    col = lax.broadcasted_iota(jnp.int32, (width, width), 1)
    for at in range(use_ref.shape[0]):
        c, j = at % pieces, at // pieces
        total_ref, other_ref = refs[c], refs[pieces + c]
        own = total_ref[j]
        other = other_ref[j]
        later = jnp.where(upper, own, other)
        if top_next:
            earlier = jnp.where(upper, other[:, width:], own[:, width:])
            total_out[at] = dot_ff(later[:, :width], earlier) + later[:, width:]
        else:
            total_out[at] = group_step(upper, own, other)
        if first:
            keep_ref, got_ref = refs[2 * pieces + c], refs[3 * pieces + c]
            passed = jnp.where(x, got_ref[j, :, :width], keep_ref[j, :, :width])
            prefix = jnp.concatenate([jnp.where(row == col, 1.0, 0.0), passed], axis=0)
            reached = jnp.concatenate([other, dot_ff(passed, other)], axis=0)
        else:
            prefix = refs[2 * pieces][at]
            reached = dot_ff(prefix, other)
        prefix_out[at] = jnp.where(upper, reached[:, :width], prefix)
        memory = jnp.where(upper, reached[:, width:], 0.0)
        use_ref[at] = jnp.where(x, memory[width:], memory[:width])
        send_ref[at] = jnp.where(x, memory[:width], memory[width:])


def top_kernel(level, pos_ref, prefix_ref, other_ref, use_ref, send_ref):
    width = other_ref.shape[1]
    upper = bit_of(pos_ref, level)
    x = bit_of(pos_ref, 1)
    for j in range(prefix_ref.shape[0]):
        memory = jnp.where(upper, dot_ff(prefix_ref[j], other_ref[j]), 0.0)
        use_ref[j] = jnp.where(x, memory[width:], memory[:width])
        send_ref[j] = jnp.where(x, memory[:width], memory[width:])


def gain_of(heads, level, j, pos_ref, cols_ref, got_ref):
    return jnp.concatenate(gate_columns(heads, level + 1, j, pos_ref, cols_ref, got_ref), axis=0)


def owned(x, j, share, mine, others):
    return jnp.where(x, others, mine) if j < share else jnp.where(x, mine, others)


def read_kernel(heads, level, top, pos_ref, eff_ref, read_ref, cols_ref, planes_ref, use_ref, got_ref, *refs):
    share, width = use_ref.shape[:2]
    low_refs, outs = (refs[: chunks + 1], refs[chunks + 1 :]) if level == 2 else ((), refs)
    x = bit_of(pos_ref, 1)
    for head in range(heads // 2):
        c, j = divmod(head, 2 * share // chunks)
        at = c + j % (share // chunks) * chunks
        memory = owned(x, j, share // chunks, use_ref[at], got_ref[at])
        gain = gain_of(heads, level, head, pos_ref, cols_ref, planes_ref)
        eff = eff_ref[head]
        if level > 2:
            outs[0][head] = read_ref[head] + gain * dot_ff(eff, memory)
        else:
            low_ref, pair_ref = low_refs[0], low_refs[1 + c]
            below = low_ref[at] if j < share // chunks else pair_ref[j - share // chunks, :, width:]
            both = dot_ff(eff, jnp.concatenate([jnp.where(x, below, 0.0), memory], axis=1))
            first = gain_of(heads, 1, head, pos_ref, cols_ref, planes_ref)
            outs[0][head] = read_ref[head] + first * both[:, :width] + gain * both[:, width:]
        if level == top - 1:
            outs[1][head] = gain_of(heads, top, head, pos_ref, cols_ref, planes_ref) * eff


def last_read_kernel(pos_ref, eff_ref, read_ref, use_ref, got_ref, keep_ref, away_ref):
    share, width = use_ref.shape[:2]
    count = keep_ref.shape[0]
    odd = bit_of(pos_ref, 0)
    x = bit_of(pos_ref, 1)
    for head in range(2 * share):
        c, j = divmod(head, 2 * share // chunks)
        at = c + j % (share // chunks) * chunks
        memory = owned(x, j, share // chunks, use_ref[at], got_ref[at])
        total = read_ref[head] + dot_ff(eff_ref[head], memory)
        lanes = slice(head * width, (head + 1) * width)
        keep_ref[:, lanes] = jnp.where(odd, total[count:], total[:count])
        away_ref[:, lanes] = jnp.where(odd, total[:count], total[count:])


def join_kernel(pos_ref, own_ref, sent_ref, keep_ref, got_ref, out_ref):
    half = out_ref.shape[1] // 2
    odd = bit_of(pos_ref, 0)
    own = keep_ref[...] + own_ref[...]
    other = got_ref[...] + sent_ref[...]
    out_ref[:, :half] = jnp.where(odd, other, own)
    out_ref[:, half:] = jnp.where(odd, own, other)


def near(*shape):
    return pltpu.VMEM(shape, f32)


def params():
    return pltpu.CompilerParams(vmem_limit_bytes=16 << 20)


def run(kernel, out_shapes, position, *arrays, name, static=()):
    held = [pltpu.with_memory_space_constraint(value, pltpu.VMEM) for value in arrays]
    return pl.pallas_call(
        lambda *refs: kernel(*static, *refs),
        out_shape=out_shapes,
        in_specs=[pl.BlockSpec(memory_space=pltpu.SMEM)]
        + [pl.BlockSpec(memory_space=pltpu.VMEM)] * len(arrays),
        compiler_params=params(),
        name=name,
    )(position, *held)


def opening(position, queries, key_rows, value_rows, write_strength, log_decay, level_gates):
    heads = write_strength.shape[0]
    count = queries.shape[0]
    arrays = (queries, key_rows, value_rows, write_strength, log_decay, level_gates)
    return pl.pallas_call(
        opening_kernel,
        out_shape=[pltpu.VMEM(value.shape, value.dtype) for value in arrays[:3]]
        + [near(3 * heads, count), near(count, count), near(heads, count, count), near(heads // 2, count, count)],
        in_specs=[pl.BlockSpec(memory_space=pltpu.SMEM)] + [pl.BlockSpec(memory_space=pl.ANY)] * 6,
        scratch_shapes=[pltpu.VMEM(value.shape, value.dtype) for value in arrays[3:]]
        + [pltpu.SemaphoreType.DMA((6,))],
        compiler_params=params(),
        name="opening",
    )(position, *[pltpu.with_memory_space_constraint(value, pltpu.HBM) for value in arrays])


def shards(queries, key_rows, value_rows, write_strength, log_decay, level_gates):
    size = lax.axis_size("ctx")
    levels = size.bit_length() - 1
    top = levels - 1
    position = lax.axis_index("ctx").astype(jnp.int32).reshape(1)
    heads = write_strength.shape[0]
    half = heads // 2
    share = half // chunks // 2
    count = queries.shape[0]
    width = queries.shape[1] // heads

    def swapped(value, bit):
        return lax.ppermute(value, "ctx", [(i, i ^ (1 << bit)) for i in range(size)])

    *tokens, columns, sent, inverse_sent = opening(
        position, queries, key_rows, value_rows, write_strength, log_decay, level_gates
    )
    got = swapped(sent, 0)
    own, inverse_own = run(
        block_kernel, [near(2 * half, count, count), near(half, count, count)],
        position, *tokens[1:], columns, name="block_own", static=(heads, True),
    )
    *pairs, low = run(
        pair_kernel,
        [near(share, width, 2 * width)] * (2 * chunks) + [near(chunks * share, width, width)],
        position, own, got, name="pair",
    )
    pairs_got = [swapped(pairs[2 * c], 1) for c in range(chunks)]
    inverse_sent, inverse_own, _ = lax.optimization_barrier((inverse_sent, inverse_own, low))
    inverses = (inverse_sent, inverse_own)
    effs, locals_ = [], []
    for mine in (False, True):
        eff, local = run(
            query_kernel, [near(half + (0 if mine else 1), count, width), near(count, half * width)],
            position, *tokens, columns, inverses[mine], name="query", static=(heads, mine),
        )
        effs.append(eff)
        locals_.append(local)
    local_sent, local_own = locals_
    eff_got = swapped(effs[0], 0)
    pairs_got[0], eff_own, local_own, local_sent = lax.optimization_barrier(
        (pairs_got[0], effs[1], local_own, local_sent)
    )
    eff, read = run(
        first_read_kernel, [near(half, 2 * count, width)] * 2,
        position, own, got, eff_own, eff_got, columns, name="read_first", static=(heads,),
    )
    totals = [
        run(quad_kernel, near(share, width, 2 * width), position, pairs[2 * c + 1], pairs_got[c], name="quad")
        for c in range(chunks)
    ]
    low, _ = lax.optimization_barrier((low, pairs_got[-1]))
    low = swapped(low, 1)
    owned_heads = chunks * share
    prefix = (*pairs[1::2], *pairs_got)
    pending = []
    for level in range(2, top):
        top_next = level == top - 1
        others = [swapped(total, level) for total in totals]
        use, send, *prefix, total = run(
            climb_kernel,
            [near(owned_heads, width, width)] * 2
            + [near(owned_heads, 2 * width, width), near(owned_heads, width, width if top_next else 2 * width)],
            position, *totals, *others, *prefix, name="climb", static=(level, top_next, len(totals)),
        )
        totals = [total]
        pending.append((level, use, send))
    other = swapped(totals[0], top)
    use, send = run(
        top_kernel, [near(owned_heads, width, width)] * 2, position, *prefix, other, name="top", static=(top,)
    )
    last_other = swapped(send, 1)
    for level, level_use, level_send in pending:
        extra = (low, *pairs_got) if level == 2 else ()
        level_other = swapped(level_send, 1)
        if level == top - 1:
            level_other, _ = lax.optimization_barrier((level_other, send))
        read, *gated = run(
            functools.partial(read_kernel, heads, level, top),
            [near(half, 2 * count, width)] * (2 if level == top - 1 else 1), position, eff, read, columns,
            eff_got, level_use, level_other, *extra, name="read",
        )
    keep, away = run(
        last_read_kernel, [near(count, half * width)] * 2,
        position, *gated, read, use, last_other, name="read_last",
    )
    return run(
        join_kernel, jax.ShapeDtypeStruct((count, heads * width), f32), position, local_own, local_sent,
        keep, swapped(away, 0), name="join",
    )


def solution(mesh):
    placed = (
        P(("groups", "ctx"), None),
        P(("groups", "ctx"), None),
        P(("groups", "ctx"), None),
        P(None, ("groups", "ctx")),
        P(None, ("groups", "ctx")),
        P(None, None, ("groups", "ctx")),
    )
    return jax.shard_map(
        shards, mesh=mesh, in_specs=placed, out_specs=P(("groups", "ctx"), None), check_vma=False
    )
```
